32 devices in a mesh: groups: 2 (over x), ctx: 16 (over z, y, core).
Axes of the slice: x: 2, y: 2, z: 4, core: 2. Of those that a mesh axis runs over, the one named last changes fastest.
Arguments:
- queries: bfloat16 [12288, 4096], P(('groups', 'ctx')), parts along dimension 0, may hold values from -12 to 12, as said below
- rotated_key_matrix: bfloat16 [12288, 1024], P(('groups', 'ctx')), parts along dimension 0, may hold values from -12 to 12, as said below
- value_matrix: bfloat16 [12288, 1024], P(('groups', 'ctx')), parts along dimension 0, may hold values from -6 to 6
- doc_blocks: int32 [16], P('groups'), parts along dimension 0, may hold values from 1 to 12, 48 in all
Outputs:
- attended: bfloat16 [12288, 4096], P(('groups', 'ctx')), parts along dimension 0
The draws below stay inside these ranges and needn't reach their ends.
There are 2 independent parts, one for each index of `groups`. The reference program is written for one: setup_inputs(seed, part) draws one part's arguments, and reference() takes and returns one part's arrays. A program takes and returns all parts, laid end to end along the dimension named above; each array names one. Nothing has to cross between parts.
Inputs may be any that keep to these rules, and one draw needn't show every extreme that they name: `queries`: custom draw: the rows of any document are full rank. `rotated_key_matrix`: custom draw. `doc_blocks`: the entries sum to 48, so every document starts at a multiple of 128 tokens and is at most 1536 tokens long; the longest has exactly that length.
All inputs are finite; a program needn't handle non-finite values.
Results may differ from the reference program's by a relative error of at most 0.0037.
Values may be sent and summed in bfloat16 or wider, within the bound.
No kernel may reach another device: no remote copies, remote signals or barrier semaphores. Data moves between devices by JAX's collectives and lax.ppermute only.
A program may use at most 128 MiB of HBM per device.

```python
import math
import jax
import jax.numpy as jnp
import numpy as np
from jax import lax

QUERY_HEADS = 32
KEY_VALUE_HEADS = 8
HEAD_WIDTH = 128
TOKENS_PER_INDEX = 384
ALIGN = 128
DOCUMENT_REACH = 4
PACKED_LENGTH = 6144
DOCS = 8
N_CTX = 16


def query_key_pair(key):
    base = jax.random.fold_in(key, 7)
    first_key, following_key = jax.random.split(base)
    queries = jnp.clip(jax.random.normal(first_key, (PACKED_LENGTH, QUERY_HEADS * HEAD_WIDTH), jnp.float32), -4.0, 4.0)
    rotated_key_matrix = jnp.clip(jax.random.normal(following_key, (PACKED_LENGTH, KEY_VALUE_HEADS * HEAD_WIDTH), jnp.float32), -4.0, 4.0)
    return (queries, rotated_key_matrix)


def draw_queries(key, part):
    return query_key_pair(key)[0].astype(jnp.bfloat16)


def draw_rotated_key_matrix(key, part):
    return query_key_pair(key)[1].astype(jnp.bfloat16)


def steps_of(stream_key, dims, cuts, low, high):
    loudness, own = 1.0, jax.random.fold_in(stream_key, 6)
    for dim, parts in cuts:
        draws = jnp.exp(jax.random.uniform(jax.random.fold_in(own, dim), (parts,), jnp.float32, low / len(cuts), high / len(cuts)))
        loudness = loudness * jnp.repeat(draws, dims[dim] // parts).reshape([-1 if axis == dim else 1 for axis in range(len(dims))])
    return loudness


def profile(count, total, most, slope):
    loads = [(1 << 20) // math.isqrt(rank ** slope) + 1 for rank in range(2, count + 1)]
    spare, given = total - most - (count - 1), [1] * (count - 1)
    while spare > 0:
        free = [i for i in range(count - 1) if given[i] < most]
        mass, left = sum([loads[i] for i in free]), spare
        for i in free:
            more = min(most - given[i], max(1, left * loads[i] // mass), spare)
            given[i] = given[i] + more
            spare = spare - more
    return np.array([most] + given)


def ragged(rng, number_of, total, limit, slope):
    if number_of == 2:
        one = jax.random.randint(rng, (), max(1, total - limit), min(limit, total - 1) + 1)
        return jnp.stack([one, total - one])
    tallies = jnp.asarray(profile(number_of, total, limit, slope), jnp.int32)
    couples = (number_of - 1) // 2
    giver, taker = tallies[1:1 + 2 * couples:2], tallies[2:2 + 2 * couples:2]
    room = jnp.minimum(giver - 1, limit - taker)
    shifted = jax.random.randint(jax.random.fold_in(rng, 1), (couples,), 0, 1 << 20) % (room + 1)
    tallies = tallies.at[1:1 + 2 * couples:2].set(giver - shifted).at[2:2 + 2 * couples:2].set(taker + shifted)
    return tallies[jax.random.permutation(jax.random.fold_in(rng, 2), number_of)]


def bell_draw(own_key, shape, width, bound, cuts=(), kind=jnp.bfloat16):
    result = jax.random.normal(own_key, shape, jnp.float32) * width
    if len(cuts) > 0:
        result = steps_of(own_key, shape, cuts, -0.22, 0.18) * result
    return jnp.clip(result, min=-bound, max=bound).astype(kind)


def setup_inputs(seed: int = 0, part: int = 0) -> dict:
    seeds = jax.random.split(jax.random.key(seed), 5)
    own_keys = jax.random.split(jax.random.fold_in(seeds[4], part), 5)
    queries = draw_queries(jax.random.fold_in(jax.random.fold_in(seeds[4], part), 71), part)
    rotated_key_matrix = draw_rotated_key_matrix(jax.random.fold_in(jax.random.fold_in(seeds[4], part), 71), part)
    value_matrix = bell_draw(own_keys[2], (PACKED_LENGTH, KEY_VALUE_HEADS * HEAD_WIDTH), 1.0, 6.0, ((0, 16),))
    doc_blocks = ragged(own_keys[3], DOCS, PACKED_LENGTH // ALIGN, DOCUMENT_REACH * TOKENS_PER_INDEX // ALIGN, 2).astype(jnp.int32)
    return {"queries": queries, "rotated_key_matrix": rotated_key_matrix, "value_matrix": value_matrix, "doc_blocks": doc_blocks}


def doc_of(positions, doc_blocks):
    doc_ends = jnp.cumsum(doc_blocks.astype(jnp.int32)).astype(jnp.int32) * ALIGN
    doc_index = jnp.sum((positions[:, None] >= doc_ends[None, :]).astype(jnp.int32), axis=1).astype(jnp.int32)
    return jnp.where(positions < 0, -1, doc_index).astype(jnp.int32)


def attend(query_block_rows, key_block_rows, value_block_rows, query_pos, key_pos, doc_blocks):
    token_row_count = query_block_rows.shape[0]
    reach_row_count = key_block_rows.shape[0]
    query_group_count = QUERY_HEADS // KEY_VALUE_HEADS
    score_scale = 1.0 / (HEAD_WIDTH ** 0.5)
    query_tensor_quad = query_block_rows.reshape(token_row_count, KEY_VALUE_HEADS, query_group_count, HEAD_WIDTH)
    key_tensor_triple = key_block_rows.reshape(reach_row_count, KEY_VALUE_HEADS, HEAD_WIDTH)
    value_tensor_triple = value_block_rows.reshape(reach_row_count, KEY_VALUE_HEADS, HEAD_WIDTH)
    query_doc = doc_of(query_pos, doc_blocks)
    key_doc = doc_of(key_pos, doc_blocks)
    allowed = (key_doc[None, :] == query_doc[:, None]) & (key_pos[None, :] <= query_pos[:, None])

    def head_split_rows(head_index):
        query_head = lax.dynamic_index_in_dim(query_tensor_quad, head_index, 1, keepdims=False)
        key_head = lax.dynamic_index_in_dim(key_tensor_triple, head_index, 1, keepdims=False)
        value_head = lax.dynamic_index_in_dim(value_tensor_triple, head_index, 1, keepdims=False)
        scores = jnp.einsum("cgd,ld->gcl", query_head.astype(jnp.float32), key_head.astype(jnp.float32)) * score_scale
        scores = jnp.where(allowed[None], scores, -1e30)
        row_max = jnp.max(scores, axis=-1, keepdims=True)
        weights = jnp.where(allowed[None], jnp.exp(scores - row_max), 0.0)
        totals = jnp.sum(weights, axis=-1)
        rounded = weights.astype(jnp.bfloat16)
        weighted = jnp.einsum("gcl,ld->cgd", rounded.astype(jnp.float32), value_head.astype(jnp.float32))
        return weighted / jnp.transpose(totals)[:, :, None]

    stacked_parts = lax.map(head_split_rows, jnp.arange(KEY_VALUE_HEADS, dtype=jnp.int32))
    return jnp.transpose(stacked_parts, (1, 0, 2, 3)).reshape(token_row_count, QUERY_HEADS * HEAD_WIDTH).astype(jnp.bfloat16)


def reference(queries, rotated_key_matrix, value_matrix, doc_blocks):
    leading_part = jnp.zeros((DOCUMENT_REACH * TOKENS_PER_INDEX, KEY_VALUE_HEADS * HEAD_WIDTH), rotated_key_matrix.dtype)
    padded_keys = jnp.concatenate([leading_part, rotated_key_matrix], axis=0)
    padded_values = jnp.concatenate([leading_part, value_matrix], axis=0)

    def per_shard(shard):
        start = (shard * TOKENS_PER_INDEX).astype(jnp.int32)
        query_block_rows = lax.dynamic_slice_in_dim(queries, start, TOKENS_PER_INDEX, 0)
        key_block_rows = lax.dynamic_slice_in_dim(padded_keys, start, (DOCUMENT_REACH + 1) * TOKENS_PER_INDEX, 0)
        value_block_rows = lax.dynamic_slice_in_dim(padded_values, start, (DOCUMENT_REACH + 1) * TOKENS_PER_INDEX, 0)
        query_pos = (start + jnp.arange(TOKENS_PER_INDEX, dtype=jnp.int32)).astype(jnp.int32)
        key_pos = (start - DOCUMENT_REACH * TOKENS_PER_INDEX + jnp.arange((DOCUMENT_REACH + 1) * TOKENS_PER_INDEX, dtype=jnp.int32)).astype(jnp.int32)
        return attend(query_block_rows, key_block_rows, value_block_rows, query_pos, key_pos, doc_blocks)

    blocks = lax.map(per_shard, jnp.arange(N_CTX, dtype=jnp.int32))
    return blocks.reshape(PACKED_LENGTH, QUERY_HEADS * HEAD_WIDTH)
```

```python
import math

import jax
import jax.numpy as jnp
from jax import lax
from jax.experimental import pallas as pl
from jax.experimental.pallas import tpu as pltpu
from jax.sharding import PartitionSpec as P

HEADS_PER_KEY = 4
WIDTH = 128
KEY_HEADS = 8
HALF = KEY_HEADS // 2
BLOCK = 128
LONGEST = 12
LOG2_SCALE = math.log2(math.e) / math.sqrt(WIDTH)
BLANK = -1e30


def permuted(array, target):
    devices = lax.axis_size("ctx")
    pairs = [(i, target(i)) for i in range(devices) if 0 <= target(i) < devices]
    return lax.ppermute(array, "ctx", pairs)


def attend_rows(width, query_ref, key_ref, value_ref, out_ref, block, low, diagonal, parts):
    heads = HEADS_PER_KEY // parts
    rows = heads * BLOCK
    first = diagonal - width + 1
    for part in range(parts):
        mine = pl.ds(part * heads, heads)
        here = pl.ds(pl.multiple_of(block * BLOCK, BLOCK), BLOCK)
        span = pl.ds(pl.multiple_of(first * BLOCK, BLOCK), width * BLOCK)
        query = query_ref[mine, here, :].reshape(rows, WIDTH)
        scores = lax.dot_general(
            query, key_ref[span, :], (((1,), (1,)), ((), ())), preferred_element_type=jnp.float32
        )
        tiles = []
        for t in range(width):
            tile = scores[:, t * BLOCK : (t + 1) * BLOCK]
            if t == width - 1:
                row = lax.broadcasted_iota(jnp.int32, (rows, BLOCK), 0) & (BLOCK - 1)
                column = lax.broadcasted_iota(jnp.int32, (rows, BLOCK), 1)
                tile = jnp.where(column <= row, tile, BLANK)
            elif t < 2:
                tile = jnp.where(jnp.broadcast_to(first + t >= low, (rows, BLOCK)), tile, BLANK)
            tiles.append(tile)
        scores = jnp.concatenate(tiles, axis=1)
        top = jnp.max(scores, axis=1, keepdims=True)
        weights = jnp.exp2((scores - top) * LOG2_SCALE)
        totals = jnp.sum(weights, axis=1, keepdims=True)
        mixed = lax.dot_general(
            weights.astype(jnp.bfloat16), value_ref[span, :], (((1,), (0,)), ((), ())),
            preferred_element_type=jnp.float32,
        )
        out_ref[mine, here, :] = (mixed / totals).astype(jnp.bfloat16).reshape(heads, BLOCK, WIDTH)


def chunk_call(head, tokens, docs, carried, parts=2):
    chip_blocks = 2 * tokens // BLOCK

    def kernel(place, doc_blocks, queries, partner_queries, near, before, far, *rest):
        if carried:
            _, returned, out, out_partner, *rest = rest
        else:
            out, out_partner, *rest = rest
        query_ref, key_ref, value_ref, done_ref, sem = rest
        chip = place[0]
        core = place[1]
        starts = []
        column = pl.multiple_of((core * HALF + head) * HEADS_PER_KEY * WIDTH, WIDTH)
        for a in range(HEADS_PER_KEY):
            starts.append(pltpu.make_async_copy(
                queries.at[:, pl.ds(pl.multiple_of(column + a * WIDTH, WIDTH), WIDTH)],
                query_ref.at[a, pl.ds(pl.multiple_of(core * tokens, BLOCK), tokens)], sem.at[0]))
            starts.append(pltpu.make_async_copy(
                partner_queries.at[:, pl.ds((head * HEADS_PER_KEY + a) * WIDTH, WIDTH)],
                query_ref.at[a, pl.ds(pl.multiple_of((1 - core) * tokens, BLOCK), tokens)], sem.at[0]))
        for slot, piece in enumerate((far, before, near)):
            for side in range(2):
                whose = core if side == 0 else 1 - core
                row = pl.multiple_of((2 * slot + whose) * tokens, BLOCK)
                starts.append(pltpu.make_async_copy(
                    piece.at[pl.ds(side * tokens, tokens), pl.ds(0, WIDTH)],
                    key_ref.at[pl.ds(row, tokens)], sem.at[0]))
                starts.append(pltpu.make_async_copy(
                    piece.at[pl.ds(side * tokens, tokens), pl.ds(WIDTH, WIDTH)],
                    value_ref.at[pl.ds(row, tokens)], sem.at[0]))
        for copy in starts:
            copy.start()
        ends = []
        if carried:
            other = pl.multiple_of(((1 - core) * HALF + head - 1) * HEADS_PER_KEY * WIDTH, WIDTH)
            ends.append(pltpu.make_async_copy(
                returned, out.at[:, pl.ds(other, HEADS_PER_KEY * WIDTH)], sem.at[2]))
            ends[0].start()
        for copy in starts:
            copy.wait()

        def one_block(block, carry):
            here = chip * chip_blocks + block

            def document(j, state):
                end, begin = state
                end = end + doc_blocks[j]
                return end, jnp.where(end <= here, end, begin)

            _, begin = lax.fori_loop(0, docs, document, (jnp.int32(0), jnp.int32(0)))
            diagonal = 2 * chip_blocks + block
            low = begin - here + diagonal
            count = diagonal - low + 1
            for width in range(3, LONGEST + 1, 3):
                @pl.when((count <= width) & (count > width - 3))
                def _():
                    attend_rows(width, query_ref, key_ref, value_ref, done_ref, block, low, diagonal, parts)
            return carry

        lax.fori_loop(0, chip_blocks, one_block, 0)
        stores = []
        for a in range(HEADS_PER_KEY):
            stores.append(pltpu.make_async_copy(
                done_ref.at[a, pl.ds(pl.multiple_of(core * tokens, BLOCK), tokens)],
                out.at[:, pl.ds(pl.multiple_of(column + a * WIDTH, WIDTH), WIDTH)], sem.at[1]))
            stores.append(pltpu.make_async_copy(
                done_ref.at[a, pl.ds(pl.multiple_of((1 - core) * tokens, BLOCK), tokens)],
                out_partner.at[:, pl.ds(a * WIDTH, WIDTH)], sem.at[1]))
        for copy in stores:
            copy.start()
        for copy in stores + ends:
            copy.wait()

    any_space = pl.BlockSpec(memory_space=pl.ANY)
    scalar = pl.BlockSpec(memory_space=pltpu.SMEM)
    inputs = 7 + (2 if carried else 0)
    return pl.pallas_call(
        kernel,
        out_shape=(
            jax.ShapeDtypeStruct((tokens, KEY_HEADS * HEADS_PER_KEY * WIDTH), jnp.bfloat16),
            jax.ShapeDtypeStruct((tokens, HEADS_PER_KEY * WIDTH), jnp.bfloat16),
        ),
        in_specs=[scalar, scalar] + [any_space] * (inputs - 2),
        out_specs=(any_space, any_space),
        scratch_shapes=[
            pltpu.VMEM((HEADS_PER_KEY, 2 * tokens, WIDTH), jnp.bfloat16),
            pltpu.VMEM((6 * tokens, WIDTH), jnp.bfloat16),
            pltpu.VMEM((6 * tokens, WIDTH), jnp.bfloat16),
            pltpu.VMEM((HEADS_PER_KEY, 2 * tokens, WIDTH), jnp.bfloat16),
            pltpu.SemaphoreType.DMA((3,)),
        ],
        input_output_aliases={7: 0} if carried else {},
        compiler_params=pltpu.CompilerParams(vmem_limit_bytes=48 << 20),
    )


def last_call(tokens):
    def kernel(place, out_in, returned, out, sem):
        other = pl.multiple_of(((1 - place[1]) * HALF + HALF - 1) * HEADS_PER_KEY * WIDTH, WIDTH)
        copy = pltpu.make_async_copy(returned, out.at[:, pl.ds(other, HEADS_PER_KEY * WIDTH)], sem)
        copy.start()
        copy.wait()

    any_space = pl.BlockSpec(memory_space=pl.ANY)
    return pl.pallas_call(
        kernel,
        out_shape=jax.ShapeDtypeStruct((tokens, KEY_HEADS * HEADS_PER_KEY * WIDTH), jnp.bfloat16),
        in_specs=[pl.BlockSpec(memory_space=pltpu.SMEM), any_space, any_space],
        out_specs=any_space,
        scratch_shapes=[pltpu.SemaphoreType.DMA(())],
        input_output_aliases={1: 0},
    )


def on_device(queries, keys, values, doc_blocks):
    tokens = queries.shape[0]
    docs = doc_blocks.shape[0]
    place = lax.axis_index("ctx")
    chip, core = place // 2, place % 2
    odd = chip % 2 == 1
    where = jnp.stack([chip, core]).astype(jnp.int32)
    half = HALF * WIDTH
    own = [lax.dynamic_slice_in_dim(x, core * half, half, 1) for x in (keys, values)]
    other = [lax.dynamic_slice_in_dim(x, (1 - core) * half, half, 1) for x in (keys, values)]
    swap = lambda x: permuted(x, lambda i: i ^ 1)
    from_partner = swap(jnp.concatenate(other, axis=1))
    other_queries = lax.dynamic_slice_in_dim(queries, (1 - core) * half * HEADS_PER_KEY, half * HEADS_PER_KEY, 1)
    partner_queries = swap(other_queries)
    chip_data = []
    for h in range(HALF):
        part = slice(h * WIDTH, (h + 1) * WIDTH)
        late = slice(half + h * WIDTH, half + (h + 1) * WIDTH)
        mine = jnp.concatenate([own[0][:, part], own[1][:, part]], axis=1)
        theirs = jnp.concatenate([from_partner[:, part], from_partner[:, late]], axis=1)
        chip_data.append(jnp.concatenate([mine, theirs], axis=0))
    far, before = [], []
    for h in range(HALF):
        far.append(permuted(chip_data[h], lambda i: i + 4))
    for h in range(HALF - 1):
        before.append(permuted(jnp.where(odd, far[h], chip_data[h]), lambda i: i ^ 2))
    before.append(permuted(chip_data[HALF - 1], lambda i: i + 2))
    out = None
    for h in range(HALF):
        call = chunk_call(h, tokens, docs, h > 0)
        extra = () if h == 0 else (out, swap(out_partner))
        out, out_partner = call(where, doc_blocks, queries, partner_queries, chip_data[h], before[h], far[h], *extra)
    return last_call(tokens)(where, out, swap(out_partner))


def solution(mesh):
    placed = (
        P(("groups", "ctx"), None),
        P(("groups", "ctx"), None),
        P(("groups", "ctx"), None),
        P("groups"),
    )
    return jax.shard_map(
        on_device, mesh=mesh, in_specs=placed, out_specs=P(("groups", "ctx"), None), check_vma=False
    )
```

```python
import math

import jax
import jax.numpy as jnp
from jax import lax
from jax.experimental import pallas as pl
from jax.experimental.pallas import tpu as pltpu
from jax.sharding import PartitionSpec as P

GROUP = 4
WIDTH = 128
KEY_HEADS = 8
HALF = KEY_HEADS // 2
BLOCK = 128
LONGEST = 12
LOG2_SCALE = math.log2(math.e) / math.sqrt(WIDTH)
BLANK = -1e30
ANY = pl.BlockSpec(memory_space=pl.ANY)
SCALAR = pl.BlockSpec(memory_space=pltpu.SMEM)


def permuted(array, target):
    devices = lax.axis_size("ctx")
    pairs = [(i, target(i)) for i in range(devices) if 0 <= target(i) < devices]
    return lax.ppermute(array, "ctx", pairs)


def aligned(x):
    return pl.multiple_of(x, 128)


def attend_rows(width, query_ref, key_ref, value_ref, out_ref, heads, block, low, diagonal):
    parts = 2
    count = GROUP // parts
    rows = count * BLOCK
    first = diagonal - width + 1
    here = pl.ds(aligned(block * BLOCK), BLOCK)
    span = pl.ds(aligned(first * BLOCK), width * BLOCK)
    units = [(h, p) for p in range(parts) for h in range(heads)]

    def score(h, p):
        query = query_ref[h, p * count : (p + 1) * count, here, :].reshape(rows, WIDTH)
        scores = lax.dot_general(
            query, key_ref[h, span, :], (((1,), (1,)), ((), ())), preferred_element_type=jnp.float32
        )
        tiles = []
        for t in range(width):
            tile = scores[:, t * BLOCK : (t + 1) * BLOCK]
            if t == width - 1:
                row = lax.broadcasted_iota(jnp.int32, (rows, BLOCK), 0) & (BLOCK - 1)
                column = lax.broadcasted_iota(jnp.int32, (rows, BLOCK), 1)
                tile = jnp.where(column <= row, tile, BLANK)
            elif t < 2:
                tile = jnp.where(jnp.broadcast_to(first + t >= low, (rows, BLOCK)), tile, BLANK)
            tiles.append(tile)
        return tiles

    def weigh(tiles):
        top = tiles[0]
        for tile in tiles[1:]:
            top = jnp.maximum(top, tile)
        top = jnp.broadcast_to(jnp.max(top, axis=1, keepdims=True), (rows, BLOCK))
        return jnp.concatenate(
            [jnp.exp2((tile - top) * LOG2_SCALE).astype(jnp.bfloat16) for tile in tiles], axis=1
        )

    def mix(h, p, weights):
        mixed = lax.dot_general(
            weights, value_ref[h, span, :], (((1,), (0,)), ((), ())), preferred_element_type=jnp.float32
        )
        done = mixed[:, :WIDTH] / mixed[:, WIDTH:]
        out_ref[h, p * count : (p + 1) * count, here, :] = done.astype(jnp.bfloat16).reshape(
            count, BLOCK, WIDTH
        )

    scores = [score(h, p) for h, p in units]
    weights = [weigh(tiles) for tiles in scores]
    for (h, p), w in zip(units, weights):
        mix(h, p, w)


def pack_call(tokens, first, heads):
    def kernel(place, keys, values, own, other, buffer, sem):
        core = place[0] % 2
        loads = []
        for o in range(2):
            half = core if o == 1 else 1 - core
            for s, source in enumerate((keys, values)):
                column = aligned((half * HALF + first) * WIDTH)
                loads.append(pltpu.make_async_copy(
                    source.at[:, pl.ds(column, heads * WIDTH)], buffer.at[o, s], sem.at[o, s]))
        stores = []
        for o, target in enumerate((other, own)):
            for s in range(2):
                stores.append(pltpu.make_async_copy(
                    buffer.at[o, s], target.at[:, pl.ds(s * heads * WIDTH, heads * WIDTH)], sem.at[o, 2 + s]))
        for copy in loads:
            copy.start()
        for load, store in zip(loads, stores):
            load.wait()
            store.start()
        for copy in stores:
            copy.wait()

    shape = jax.ShapeDtypeStruct((tokens, 2 * heads * WIDTH), jnp.bfloat16)
    return pl.pallas_call(
        kernel,
        out_shape=(shape, shape),
        in_specs=[SCALAR, ANY, ANY],
        out_specs=(ANY, ANY),
        scratch_shapes=[
            pltpu.VMEM((2, 2, tokens, heads * WIDTH), jnp.bfloat16),
            pltpu.SemaphoreType.DMA((2, 4)),
        ],
    )


def chunk_call(first, heads, tokens, docs, carried):
    chip_blocks = 2 * tokens // BLOCK
    pieces = 6

    def kernel(place, doc_blocks, queries, partner_queries, *rest):
        sides, rest = rest[:pieces], rest[pieces:]
        if carried:
            rest = rest[1:]
        out, out_partner, *rest = rest
        query_ref, key_ref, value_ref, done_ref, sem = rest
        chip = place[0] // 2
        core = place[0] % 2
        mine = [aligned(core * tokens), aligned((1 - core) * tokens)]
        column = (core * HALF + first) * GROUP * WIDTH
        loads = []
        for h in range(heads):
            for a in range(GROUP):
                at = aligned(column + (h * GROUP + a) * WIDTH)
                for side, source in enumerate((queries, partner_queries)):
                    loads.append(pltpu.make_async_copy(
                        source.at[:, pl.ds(at, WIDTH)],
                        query_ref.at[h, a, pl.ds(mine[side], tokens)], sem.at[0]))
        for slot in range(3):
            for side in range(2):
                piece = sides[2 * slot + side]
                to = pl.ds(aligned(2 * slot * tokens + mine[side]), tokens)
                for h in range(heads):
                    loads.append(pltpu.make_async_copy(
                        piece.at[:, pl.ds(h * WIDTH, WIDTH)], key_ref.at[h, to], sem.at[0]))
                    loads.append(pltpu.make_async_copy(
                        piece.at[:, pl.ds((heads + h) * WIDTH, WIDTH)],
                        value_ref.at[h, to, pl.ds(0, WIDTH)], sem.at[0]))
        for copy in loads:
            copy.start()
        for h in range(heads):
            value_ref[h, :, WIDTH:] = jnp.ones((6 * tokens, WIDTH), jnp.bfloat16)
        for copy in loads:
            copy.wait()

        def one_block(block, carry):
            here = chip * chip_blocks + block

            def document(j, state):
                end, begin = state
                end = end + doc_blocks[j]
                return end, jnp.where(end <= here, end, begin)

            _, begin = lax.fori_loop(0, docs, document, (jnp.int32(0), jnp.int32(0)))
            diagonal = 2 * chip_blocks + block
            low = begin - here + diagonal
            count = diagonal - low + 1
            for width in range(3, LONGEST + 1, 3):
                @pl.when((count <= width) & (count > width - 3))
                def _():
                    attend_rows(width, query_ref, key_ref, value_ref, done_ref, heads, block, low, diagonal)
            return carry

        lax.fori_loop(0, chip_blocks, one_block, 0)
        stores = []
        for h in range(heads):
            for a in range(GROUP):
                at = aligned(column + (h * GROUP + a) * WIDTH)
                stores.append(pltpu.make_async_copy(
                    done_ref.at[h, a, pl.ds(mine[1], tokens)],
                    out_partner.at[:, pl.ds((h * GROUP + a) * WIDTH, WIDTH)], sem.at[1]))
                stores.append(pltpu.make_async_copy(
                    done_ref.at[h, a, pl.ds(mine[0], tokens)], out.at[:, pl.ds(at, WIDTH)], sem.at[1]))
        for copy in stores:
            copy.start()
        for copy in stores:
            copy.wait()

    inputs = 4 + pieces
    return pl.pallas_call(
        kernel,
        out_shape=(
            jax.ShapeDtypeStruct((tokens, KEY_HEADS * GROUP * WIDTH), jnp.bfloat16),
            jax.ShapeDtypeStruct((tokens, heads * GROUP * WIDTH), jnp.bfloat16),
        ),
        in_specs=[SCALAR, SCALAR] + [ANY] * (inputs - 2 + carried),
        out_specs=(ANY, ANY),
        scratch_shapes=[
            pltpu.VMEM((heads, GROUP, 2 * tokens, WIDTH), jnp.bfloat16),
            pltpu.VMEM((heads, 6 * tokens, WIDTH), jnp.bfloat16),
            pltpu.VMEM((heads, 6 * tokens, 2 * WIDTH), jnp.bfloat16),
            pltpu.VMEM((heads, GROUP, 2 * tokens, WIDTH), jnp.bfloat16),
            pltpu.SemaphoreType.DMA((2,)),
        ],
        input_output_aliases={inputs: 0} if carried else {},
        compiler_params=pltpu.CompilerParams(vmem_limit_bytes=48 << 20),
        cost_estimate=pl.CostEstimate(
            flops=heads * 5_000_000_000, transcendentals=0, bytes_accessed=heads * 4_000_000),
    )


def last_call(tokens, heads):
    width = heads * GROUP * WIDTH

    def kernel(place, out_in, *rest):
        *returned, out, sem = rest
        copies = []
        for part, source in enumerate(returned):
            other = aligned(((1 - place[0] % 2) * HALF + part * heads) * GROUP * WIDTH)
            copies.append(pltpu.make_async_copy(source, out.at[:, pl.ds(other, width)], sem.at[part]))
            copies[part].start()
        for copy in copies:
            copy.wait()

    return pl.pallas_call(
        kernel,
        out_shape=jax.ShapeDtypeStruct((tokens, KEY_HEADS * GROUP * WIDTH), jnp.bfloat16),
        in_specs=[SCALAR, ANY] + [pl.BlockSpec(memory_space=pltpu.VMEM)] * (HALF // heads),
        out_specs=ANY,
        scratch_shapes=[pltpu.SemaphoreType.DMA((HALF // heads,))],
        input_output_aliases={1: 0},
        compiler_params=pltpu.CompilerParams(vmem_limit_bytes=32 << 20),
    )


def on_device(queries, keys, values, doc_blocks):
    tokens = queries.shape[0]
    docs = doc_blocks.shape[0]
    place = lax.axis_index("ctx").astype(jnp.int32)
    odd = (place // 2) % 2 == 1
    place = place.reshape(1)
    swap = lambda x: permuted(x, lambda i: i ^ 1)
    hop = lambda x: permuted(x, lambda i: i + 4)
    across = lambda x: permuted(x, lambda i: i ^ 2)

    own, other = pack_call(tokens, 0, 2)(place, keys, values)
    received = swap(other)
    keys, own = lax.optimization_barrier((keys, own))
    own_late, other_late = pack_call(tokens, 2, 2)(place, keys, values)
    other_late, received = lax.optimization_barrier((other_late, received))
    received_late = swap(other_late)
    queries, received_late = lax.optimization_barrier((queries, received_late))
    partner_queries = swap(queries)
    near = [own, received, own_late, received_late]
    far = [hop(x) for x in near]
    before = [across(jnp.where(odd, f, n)) for n, f in zip(near[:3], far[:3])]
    before.append(permuted(received_late, lambda i: i + 2))
    before[1], far[2] = lax.optimization_barrier((before[1], far[2]))
    out, partner = chunk_call(0, 2, tokens, docs, False)(
        place, doc_blocks, queries, partner_queries, *far[:2], *before[:2], *near[:2])
    out, partner_late = chunk_call(2, 2, tokens, docs, True)(
        place, doc_blocks, queries, partner_queries, *far[2:], *before[2:], *near[2:], out)
    return last_call(tokens, 2)(place, out, swap(partner), swap(partner_late))


def solution(mesh):
    placed = (
        P(("groups", "ctx"), None),
        P(("groups", "ctx"), None),
        P(("groups", "ctx"), None),
        P("groups"),
    )
    return jax.shard_map(
        on_device, mesh=mesh, in_specs=placed, out_specs=P(("groups", "ctx"), None), check_vma=False
    )
```

```python
import math

import jax
import jax.numpy as jnp
from jax import lax
from jax.experimental import pallas as pl
from jax.experimental.pallas import tpu as pltpu
from jax.sharding import PartitionSpec as P

GROUP = 4
WIDTH = 128
KEY_HEADS = 8
HALF = KEY_HEADS // 2
BLOCK = 128
LONGEST = 12
LOG2_SCALE = math.log2(math.e) / math.sqrt(WIDTH)
BLANK = -1e30
ANY = pl.BlockSpec(memory_space=pl.ANY)
SCALAR = pl.BlockSpec(memory_space=pltpu.SMEM)


def permuted(array, target):
    devices = lax.axis_size("ctx")
    pairs = [(i, target(i)) for i in range(devices) if 0 <= target(i) < devices]
    return lax.ppermute(array, "ctx", pairs)


def aligned(x):
    return pl.multiple_of(x, 128)


def scores_of(query, key, first, low, diagonal):
    rows = query.shape[0]
    width = key.shape[0] // BLOCK
    scores = lax.dot_general(query, key, (((1,), (1,)), ((), ())), preferred_element_type=jnp.float32)
    tiles = []
    for t in range(width):
        tile = scores[:, t * BLOCK : (t + 1) * BLOCK]
        if diagonal and t == width - 1:
            row = lax.broadcasted_iota(jnp.int32, (rows, BLOCK), 0) & (BLOCK - 1)
            column = lax.broadcasted_iota(jnp.int32, (rows, BLOCK), 1)
            tile = jnp.where(column <= row, tile, BLANK)
        elif t < 2:
            tile = jnp.where(jnp.broadcast_to(first + t >= low, (rows, BLOCK)), tile, BLANK)
        tiles.append(tile)
    return tiles


def attend_block(width, heads, query_ref, pair_ref, block, row, first, low, diagonal, before, after):
    parts = 2
    count = GROUP // parts
    rows = count * BLOCK
    here = pl.ds(aligned(block * BLOCK), BLOCK)
    span = pl.ds(aligned(row), width * BLOCK)
    units = [(h, p) for p in range(parts) for h in range(heads)]

    def score(h, p):
        query = jnp.concatenate(
            [query_ref[here, pl.ds((h * GROUP + p * count + a) * WIDTH, WIDTH)] for a in range(count)], axis=0)
        return scores_of(query, pair_ref[span, pl.ds(h * WIDTH, WIDTH)], first, low, diagonal)

    def weigh(tiles, past):
        top = tiles[0]
        for tile in tiles[1:]:
            top = jnp.maximum(top, tile)
        top = jnp.broadcast_to(jnp.max(top, axis=1, keepdims=True), (rows, BLOCK)) * LOG2_SCALE
        if past is not None:
            top = jnp.maximum(top, past)
        weights = [jnp.exp2(tile * LOG2_SCALE - top).astype(jnp.bfloat16) for tile in tiles]
        return jnp.concatenate(weights, axis=1), top

    def mix(h, weights):
        value = pair_ref[span, pl.ds((heads + h) * WIDTH, WIDTH)]
        value = jnp.concatenate([value, jnp.ones((width * BLOCK, WIDTH), jnp.bfloat16)], axis=1)
        mixed = lax.dot_general(weights, value, (((1,), (0,)), ((), ())), preferred_element_type=jnp.float32)
        return mixed[:, :WIDTH], mixed[:, WIDTH:]

    tiles = [score(*unit) for unit in units]
    past = [before(h, slice(p * count, (p + 1) * count), here) for h, p in units]
    weighed = [weigh(t, None if b is None else b[1]) for t, b in zip(tiles, past)]
    for (h, p), (weights, top), b in zip(units, weighed, past):
        after(h, p * count, count, here, top, *mix(h, weights), b)


def document_start(doc_blocks, docs, here):
    def document(j, state):
        end, begin = state
        end = end + doc_blocks[j]
        return end, jnp.where(end <= here, end, begin)

    return lax.fori_loop(0, docs, document, (jnp.int32(0), jnp.int32(0)))[1]


def pack_call(tokens, first, heads):
    def kernel(place, keys, values, own, other, buffer, sem):
        core = place[0] % 2
        loads = []
        for o in range(2):
            half = core if o == 1 else 1 - core
            for s, source in enumerate((keys, values)):
                column = aligned((half * HALF + first) * WIDTH)
                loads.append(pltpu.make_async_copy(
                    source.at[:, pl.ds(column, heads * WIDTH)], buffer.at[o, s], sem.at[o, s]))
        stores = []
        for o, target in enumerate((other, own)):
            for s in range(2):
                stores.append(pltpu.make_async_copy(
                    buffer.at[o, s], target.at[:, pl.ds(s * heads * WIDTH, heads * WIDTH)], sem.at[o, 2 + s]))
        for copy in loads:
            copy.start()
        for load, store in zip(loads, stores):
            load.wait()
            store.start()
        for copy in stores:
            copy.wait()

    shape = jax.ShapeDtypeStruct((tokens, 2 * heads * WIDTH), jnp.bfloat16)
    return pl.pallas_call(
        kernel,
        out_shape=(shape, shape),
        in_specs=[SCALAR, ANY, ANY],
        out_specs=(ANY, ANY),
        scratch_shapes=[
            pltpu.VMEM((2, 2, tokens, heads * WIDTH), jnp.bfloat16),
            pltpu.SemaphoreType.DMA((2, 4)),
        ],
    )


def query_loads(queries, partner_queries, query_ref, place, first, heads, tokens, sem):
    core = place[0] % 2
    columns = pl.ds(aligned((core * HALF + first) * GROUP * WIDTH), heads * GROUP * WIDTH)
    return [
        pltpu.make_async_copy(
            source.at[:, columns], query_ref.at[pl.ds(aligned((core if side == 0 else 1 - core) * tokens), tokens)], sem)
        for side, source in enumerate((queries, partner_queries))
    ]


def near_call(first, heads, tokens, docs):
    blocks = 2 * tokens // BLOCK
    pad = 2 * BLOCK

    def kernel(place, doc_blocks, queries, partner_queries, own, received, mix_out, log_out,
               query_ref, pair_ref, mix_ref, log_ref, load_sem, store_sem):
        chip = place[0] // 2
        core = place[0] % 2
        loads = query_loads(queries, partner_queries, query_ref, place, first, heads, tokens, load_sem)
        for side, piece in enumerate((own, received)):
            row = aligned(pad + (core if side == 0 else 1 - core) * tokens)
            loads.append(pltpu.make_async_copy(piece, pair_ref.at[pl.ds(row, tokens)], load_sem))
        for copy in loads:
            copy.start()
        pair_ref[:pad, :] = jnp.zeros((pad, 2 * heads * WIDTH), jnp.bfloat16)
        for copy in loads:
            copy.wait()

        def stores(block):
            here = pl.ds(aligned(block * BLOCK), BLOCK)
            return [
                pltpu.make_async_copy(mix_ref.at[:, :, here], mix_out.at[:, :, here], store_sem),
                pltpu.make_async_copy(log_ref.at[:, :, here], log_out.at[:, :, here], store_sem),
            ]

        def before(h, heads_of, here):
            return None

        def after(h, at, count, here, top, mixed, total, past):
            mix_ref[h, at : at + count, here, :] = (mixed / total).reshape(count, BLOCK, WIDTH)
            log_ref[h, at : at + count, here, :] = (top + jnp.log2(total)).reshape(count, BLOCK, WIDTH)

        def one_block(block, carry):
            here = chip * blocks + block
            low = jnp.maximum(document_start(doc_blocks, docs, here) - chip * blocks, 0)
            count = block - low + 1
            for width in range(3, blocks + 1, 3):
                @pl.when((count <= width) & (count > width - 3))
                def _():
                    start = block - width + 1
                    attend_block(width, heads, query_ref, pair_ref, block, pad + start * BLOCK, start, low, True,
                                 before, after)
            for copy in stores(block):
                copy.start()
            return carry

        lax.fori_loop(0, blocks, one_block, 0)

        def finish(block, carry):
            for copy in stores(block):
                copy.wait()
            return carry

        lax.fori_loop(0, blocks, finish, 0)

    state = jax.ShapeDtypeStruct((heads, GROUP, 2 * tokens, WIDTH), jnp.float32)
    return pl.pallas_call(
        kernel,
        out_shape=(state, state),
        in_specs=[SCALAR, SCALAR] + [ANY] * 4,
        out_specs=(ANY, ANY),
        scratch_shapes=[
            pltpu.VMEM((2 * tokens, heads * GROUP * WIDTH), jnp.bfloat16),
            pltpu.VMEM((pad + 2 * tokens, 2 * heads * WIDTH), jnp.bfloat16),
            pltpu.VMEM(state.shape, jnp.float32),
            pltpu.VMEM(state.shape, jnp.float32),
            pltpu.SemaphoreType.DMA(()),
            pltpu.SemaphoreType.DMA(()),
        ],
        compiler_params=pltpu.CompilerParams(vmem_limit_bytes=20 << 20),
        cost_estimate=pl.CostEstimate(flops=heads * 3_000_000_000, transcendentals=0, bytes_accessed=8_000_000),
    )


def far_call(first, heads, tokens, docs, carried):
    blocks = 2 * tokens // BLOCK

    def kernel(place, doc_blocks, queries, partner_queries, mix_in, log_in, *rest):
        pieces, rest = rest[:4], rest[4 + carried :]
        out, out_partner, query_ref, pair_ref, mix_ref, log_ref, done_ref, load_sem, state_sem, store_sem = rest
        chip = place[0] // 2
        core = place[0] % 2
        columns = pl.ds(aligned((core * HALF + first) * GROUP * WIDTH), heads * GROUP * WIDTH)
        loads = query_loads(queries, partner_queries, query_ref, place, first, heads, tokens, load_sem)
        for n, piece in enumerate(pieces):
            row = aligned((2 * (n // 2) + (core if n % 2 == 0 else 1 - core)) * tokens)
            loads.append(pltpu.make_async_copy(piece, pair_ref.at[pl.ds(row, tokens)], load_sem))

        def states(block):
            here = pl.ds(aligned(block * BLOCK), BLOCK)
            return [
                pltpu.make_async_copy(mix_in.at[:, :, here], mix_ref.at[:, :, here], state_sem.at[block]),
                pltpu.make_async_copy(log_in.at[:, :, here], log_ref.at[:, :, here], state_sem.at[block]),
            ]

        def store(block):
            here = pl.ds(aligned(block * BLOCK), BLOCK)
            own = block // (blocks // 2) == core
            to = pl.ds(aligned(block % (blocks // 2) * BLOCK), BLOCK)
            mine = pltpu.make_async_copy(done_ref.at[here], out.at[to, columns], store_sem)
            other = pltpu.make_async_copy(done_ref.at[here], out_partner.at[to], store_sem)
            return own, mine, other

        for copy in loads:
            copy.start()
        for block in range(blocks):
            for copy in states(block):
                copy.start()
        for copy in loads:
            copy.wait()

        def before(h, heads_of, here):
            rows = (heads_of.stop - heads_of.start) * BLOCK
            return (mix_ref[h, heads_of, here, :].reshape(rows, WIDTH), log_ref[h, heads_of, here, :].reshape(rows, WIDTH))

        def after(h, at, count, here, top, mixed, total, past):
            factor = jnp.exp2(past[1] - top)
            done = ((past[0] * factor + mixed) / (total + factor)).astype(jnp.bfloat16)
            for a in range(count):
                done_ref[here, pl.ds((h * GROUP + at + a) * WIDTH, WIDTH)] = done[a * BLOCK : (a + 1) * BLOCK]

        def one_block(block, carry):
            for copy in states(block):
                copy.wait()
            low = document_start(doc_blocks, docs, chip * blocks + block) - (chip - 2) * blocks
            count = 2 * blocks - low
            least = 0
            for width in (3, 6, 9, LONGEST - 1):
                @pl.when((count <= width) & (count > least))
                def _():
                    start = 2 * blocks - width
                    attend_block(width, heads, query_ref, pair_ref, block, start * BLOCK, start, low, False,
                                 before, after)
                least = width

            @pl.when(count <= 0)
            def _():
                here = pl.ds(aligned(block * BLOCK), BLOCK)
                for h in range(heads):
                    for a in range(GROUP):
                        done_ref[here, pl.ds((h * GROUP + a) * WIDTH, WIDTH)] = (
                            mix_ref[h, a, here, :].astype(jnp.bfloat16))

            own, mine, other = store(block)

            @pl.when(own)
            def _():
                mine.start()

            @pl.when(jnp.logical_not(own))
            def _():
                other.start()

            return carry

        lax.fori_loop(0, blocks, one_block, 0)

        def finish(block, carry):
            own, mine, other = store(block)

            @pl.when(own)
            def _():
                mine.wait()

            @pl.when(jnp.logical_not(own))
            def _():
                other.wait()

            return carry

        lax.fori_loop(0, blocks, finish, 0)

    state = (heads, GROUP, 2 * tokens, WIDTH)
    return pl.pallas_call(
        kernel,
        out_shape=(
            jax.ShapeDtypeStruct((tokens, KEY_HEADS * GROUP * WIDTH), jnp.bfloat16),
            jax.ShapeDtypeStruct((tokens, heads * GROUP * WIDTH), jnp.bfloat16),
        ),
        in_specs=[SCALAR, SCALAR] + [ANY] * (8 + carried),
        out_specs=(ANY, ANY),
        scratch_shapes=[
            pltpu.VMEM((2 * tokens, heads * GROUP * WIDTH), jnp.bfloat16),
            pltpu.VMEM((4 * tokens, 2 * heads * WIDTH), jnp.bfloat16),
            pltpu.VMEM(state, jnp.float32),
            pltpu.VMEM(state, jnp.float32),
            pltpu.VMEM((2 * tokens, heads * GROUP * WIDTH), jnp.bfloat16),
            pltpu.SemaphoreType.DMA(()),
            pltpu.SemaphoreType.DMA((blocks,)),
            pltpu.SemaphoreType.DMA(()),
        ],
        input_output_aliases={10: 0} if carried else {},
        compiler_params=pltpu.CompilerParams(vmem_limit_bytes=28 << 20),
        cost_estimate=pl.CostEstimate(flops=heads * 4_000_000_000, transcendentals=0, bytes_accessed=8_000_000),
    )


def last_call(tokens, heads):
    width = heads * GROUP * WIDTH

    def kernel(place, out_in, *rest):
        *returned, out, sem = rest
        copies = []
        for part, source in enumerate(returned):
            other = aligned(((1 - place[0] % 2) * HALF + part * heads) * GROUP * WIDTH)
            copies.append(pltpu.make_async_copy(source, out.at[:, pl.ds(other, width)], sem.at[part]))
            copies[part].start()
        for copy in copies:
            copy.wait()

    return pl.pallas_call(
        kernel,
        out_shape=jax.ShapeDtypeStruct((tokens, KEY_HEADS * GROUP * WIDTH), jnp.bfloat16),
        in_specs=[SCALAR, ANY] + [pl.BlockSpec(memory_space=pltpu.VMEM)] * (HALF // heads),
        out_specs=ANY,
        scratch_shapes=[pltpu.SemaphoreType.DMA((HALF // heads,))],
        input_output_aliases={1: 0},
        compiler_params=pltpu.CompilerParams(vmem_limit_bytes=8 << 20),
    )


def on_device(queries, keys, values, doc_blocks):
    tokens = queries.shape[0]
    docs = doc_blocks.shape[0]
    place = lax.axis_index("ctx").astype(jnp.int32)
    odd = (place // 2) % 2 == 1
    place = place.reshape(1)
    swap = lambda x: permuted(x, lambda i: i ^ 1)
    hop = lambda x: permuted(x, lambda i: i + 4)
    across = lambda x: permuted(x, lambda i: i ^ 2)

    own, other = pack_call(tokens, 0, 2)(place, keys, values)
    received = swap(other)
    keys, own = lax.optimization_barrier((keys, own))
    own_late, other_late = pack_call(tokens, 2, 2)(place, keys, values)
    other_late, received = lax.optimization_barrier((other_late, received))
    received_late = swap(other_late)
    queries, received_late = lax.optimization_barrier((queries, received_late))
    partner_queries = swap(queries)
    near = [own, received, own_late, received_late]
    far = [hop(near[0]), hop(near[1])]
    late, far[0] = lax.optimization_barrier((near[2], far[0]))
    far += [hop(late), hop(near[3])]
    common = (place, doc_blocks, queries, partner_queries)
    relay = lambda n: across(jnp.where(odd, far[n], near[n]))
    before = [relay(0)]
    state = near_call(0, 2, tokens, docs)(*common, *near[:2])
    far[1], *state = lax.optimization_barrier((far[1], *state))
    before.append(relay(1))
    state_late = near_call(2, 2, tokens, docs)(*common, *near[2:])
    far[2], *state_late = lax.optimization_barrier((far[2], *state_late))
    before.append(relay(2))
    before.append(permuted(received_late, lambda i: i + 2))
    before[1], far[2] = lax.optimization_barrier((before[1], far[2]))
    out, partner = far_call(0, 2, tokens, docs, False)(*common, *state, *far[:2], *before[:2])
    out, partner_late = far_call(2, 2, tokens, docs, True)(*common, *state_late, *far[2:], *before[2:], out)
    return last_call(tokens, 2)(place, out, swap(partner), swap(partner_late))


def solution(mesh):
    placed = (
        P(("groups", "ctx"), None),
        P(("groups", "ctx"), None),
        P(("groups", "ctx"), None),
        P("groups"),
    )
    return jax.shard_map(
        on_device, mesh=mesh, in_specs=placed, out_specs=P(("groups", "ctx"), None), check_vma=False
    )
```

```python
import math

import jax
import jax.numpy as jnp
from jax import lax
from jax.experimental import pallas as pl
from jax.experimental.pallas import tpu as pltpu
from jax.sharding import PartitionSpec as P

GROUP = 4
WIDTH = 128
KEY_HEADS = 8
HALF = KEY_HEADS // 2
BLOCK = 128
LONGEST = 12
LOG2_SCALE = math.log2(math.e) / math.sqrt(WIDTH)
BLANK = -1e30
ANY = pl.BlockSpec(memory_space=pl.ANY)
HBM = pl.BlockSpec(memory_space=pltpu.HBM)
SCALAR = pl.BlockSpec(memory_space=pltpu.SMEM)


def permuted(array, target):
    devices = lax.axis_size("ctx")
    pairs = [(i, target(i)) for i in range(devices) if 0 <= target(i) < devices]
    return lax.ppermute(array, "ctx", pairs)


def aligned(x):
    return pl.multiple_of(x, 128)


def scores_of(query, key, first, low, diagonal):
    rows = query.shape[0]
    width = key.shape[0] // BLOCK
    scores = lax.dot_general(query, key, (((1,), (1,)), ((), ())), preferred_element_type=jnp.float32)
    tiles = []
    for t in range(width):
        tile = scores[:, t * BLOCK : (t + 1) * BLOCK]
        if diagonal and t == width - 1:
            row = lax.broadcasted_iota(jnp.int32, (rows, BLOCK), 0) & (BLOCK - 1)
            column = lax.broadcasted_iota(jnp.int32, (rows, BLOCK), 1)
            tile = jnp.where(column <= row, tile, BLANK)
        elif t < 2:
            tile = jnp.where(jnp.broadcast_to(first + t >= low, (rows, BLOCK)), tile, BLANK)
        tiles.append(tile)
    return tiles


def attend_block(width, heads, query_ref, pair_ref, block, row, first, low, diagonal, before, after):
    parts = 2
    count = GROUP // parts
    rows = count * BLOCK
    here = pl.ds(aligned(block * BLOCK), BLOCK)
    span = pl.ds(aligned(row), width * BLOCK)
    units = [(h, p) for p in range(parts) for h in range(heads)]

    def score(h, p):
        query = jnp.concatenate(
            [query_ref[here, pl.ds((h * GROUP + p * count + a) * WIDTH, WIDTH)] for a in range(count)], axis=0)
        return scores_of(query, pair_ref[span, pl.ds(h * WIDTH, WIDTH)], first, low, diagonal)

    def weigh(tiles, past):
        top = tiles[0]
        for tile in tiles[1:]:
            top = jnp.maximum(top, tile)
        top = jnp.broadcast_to(jnp.max(top, axis=1, keepdims=True), (rows, BLOCK)) * LOG2_SCALE
        if past is not None:
            top = jnp.maximum(top, past)
        weights = [jnp.exp2(tile * LOG2_SCALE - top).astype(jnp.bfloat16) for tile in tiles]
        return jnp.concatenate(weights, axis=1), top

    def mix(h, weights):
        value = pair_ref[span, pl.ds((heads + h) * WIDTH, WIDTH)]
        value = jnp.concatenate([value, jnp.ones((width * BLOCK, WIDTH), jnp.bfloat16)], axis=1)
        mixed = lax.dot_general(weights, value, (((1,), (0,)), ((), ())), preferred_element_type=jnp.float32)
        return mixed[:, :WIDTH], mixed[:, WIDTH:]

    tiles = [score(*unit) for unit in units]
    past = [before(h, slice(p * count, (p + 1) * count), here) for h, p in units]
    weighed = [weigh(t, None if b is None else b[1]) for t, b in zip(tiles, past)]
    for (h, p), (weights, top), b in zip(units, weighed, past):
        after(h, p * count, count, here, top, *mix(h, weights), b)


def document_start(doc_blocks, docs, here):
    def document(j, state):
        end, begin = state
        end = end + doc_blocks[j]
        return end, jnp.where(end <= here, end, begin)

    return lax.fori_loop(0, docs, document, (jnp.int32(0), jnp.int32(0)))[1]


def pack_call(tokens, heads):
    count = HALF // heads

    def kernel(place, keys, values, *rest):
        targets, buffer, load_sem, store_sem = rest[: 2 * count], *rest[2 * count :]
        core = place[0] % 2
        loads, stores = [], []
        for part in range(count):
            for o in range(2):
                half = core if o == 1 else 1 - core
                for s, source in enumerate((keys, values)):
                    column = aligned((half * HALF + part * heads) * WIDTH)
                    to = pl.ds(s * heads * WIDTH, heads * WIDTH)
                    n = part * 2 + o
                    loads.append(pltpu.make_async_copy(
                        source.at[:, pl.ds(column, heads * WIDTH)], buffer.at[n, :, to], load_sem.at[n]))
                stores.append(pltpu.make_async_copy(buffer.at[n], targets[n], store_sem))
        for copy in loads:
            copy.start()
        for n, copy in enumerate(stores):
            loads[2 * n].wait()
            loads[2 * n + 1].wait()
            copy.start()
        for copy in stores:
            copy.wait()

    shape = jax.ShapeDtypeStruct((tokens, 2 * heads * WIDTH), jnp.bfloat16)
    return pl.pallas_call(
        kernel,
        out_shape=[shape] * (2 * count),
        in_specs=[SCALAR, HBM, HBM],
        out_specs=[HBM] * (2 * count),
        scratch_shapes=[
            pltpu.VMEM((2 * count, tokens, 2 * heads * WIDTH), jnp.bfloat16),
            pltpu.SemaphoreType.DMA((2 * count,)),
            pltpu.SemaphoreType.DMA(()),
        ],
    )


def query_loads(queries, partner_queries, query_ref, place, first, heads, tokens, sem):
    core = place[0] % 2
    columns = pl.ds(aligned((core * HALF + first) * GROUP * WIDTH), heads * GROUP * WIDTH)
    return [
        pltpu.make_async_copy(
            source.at[:, columns], query_ref.at[pl.ds(aligned((core if side == 0 else 1 - core) * tokens), tokens)], sem)
        for side, source in enumerate((queries, partner_queries))
    ]


def near_call(first, heads, tokens, docs):
    blocks = 2 * tokens // BLOCK
    pad = 2 * BLOCK

    def kernel(place, doc_blocks, queries, partner_queries, own, received, mix_out, log_out,
               query_ref, pair_ref, mix_ref, log_ref, load_sem, store_sem):
        chip = place[0] // 2
        core = place[0] % 2
        loads = query_loads(queries, partner_queries, query_ref, place, first, heads, tokens, load_sem)
        for side, piece in enumerate((own, received)):
            row = aligned(pad + (core if side == 0 else 1 - core) * tokens)
            loads.append(pltpu.make_async_copy(piece, pair_ref.at[pl.ds(row, tokens)], load_sem))
        for copy in loads:
            copy.start()
        pair_ref[:pad, :] = jnp.zeros((pad, 2 * heads * WIDTH), jnp.bfloat16)
        for copy in loads:
            copy.wait()

        def stores(block):
            here = pl.ds(aligned(block * BLOCK), BLOCK)
            return [
                pltpu.make_async_copy(mix_ref.at[:, :, here], mix_out.at[:, :, here], store_sem),
                pltpu.make_async_copy(log_ref.at[:, :, here], log_out.at[:, :, here], store_sem),
            ]

        def before(h, heads_of, here):
            return None

        def after(h, at, count, here, top, mixed, total, past):
            mix_ref[h, at : at + count, here, :] = (mixed / total).reshape(count, BLOCK, WIDTH)
            log_ref[h, at : at + count, here, :] = (top + jnp.log2(total)).reshape(count, BLOCK, WIDTH)

        def one_block(block, carry):
            here = chip * blocks + block
            low = jnp.maximum(document_start(doc_blocks, docs, here) - chip * blocks, 0)
            count = block - low + 1
            for width in range(3, blocks + 1, 3):
                @pl.when((count <= width) & (count > width - 3))
                def _():
                    start = block - width + 1
                    attend_block(width, heads, query_ref, pair_ref, block, pad + start * BLOCK, start, low, True,
                                 before, after)
            for copy in stores(block):
                copy.start()
            return carry

        lax.fori_loop(0, blocks, one_block, 0)

        def finish(block, carry):
            for copy in stores(block):
                copy.wait()
            return carry

        lax.fori_loop(0, blocks, finish, 0)

    state = jax.ShapeDtypeStruct((heads, GROUP, 2 * tokens, WIDTH), jnp.float32)
    return pl.pallas_call(
        kernel,
        out_shape=(state, state),
        in_specs=[SCALAR, SCALAR] + [HBM] * 4,
        out_specs=(ANY, ANY),
        scratch_shapes=[
            pltpu.VMEM((2 * tokens, heads * GROUP * WIDTH), jnp.bfloat16),
            pltpu.VMEM((pad + 2 * tokens, 2 * heads * WIDTH), jnp.bfloat16),
            pltpu.VMEM(state.shape, jnp.float32),
            pltpu.VMEM(state.shape, jnp.float32),
            pltpu.SemaphoreType.DMA(()),
            pltpu.SemaphoreType.DMA(()),
        ],
        compiler_params=pltpu.CompilerParams(vmem_limit_bytes=20 << 20),
        cost_estimate=pl.CostEstimate(flops=heads * 3_000_000_000, transcendentals=0, bytes_accessed=8_000_000),
    )


def far_call(first, heads, tokens, docs, whole, carried):
    blocks = 2 * tokens // BLOCK
    slots = 3 if whole else 2
    states_in = 0 if whole else 2

    def kernel(place, doc_blocks, queries, partner_queries, *rest):
        state_in, rest = rest[:states_in], rest[states_in:]
        pieces, rest = rest[: 2 * slots], rest[2 * slots + carried :]
        out, out_partner, query_ref, pair_ref, done_ref, load_sem, store_sem, *rest = rest
        state_refs, state_sem = rest[:states_in], rest[-1]
        chip = place[0] // 2
        core = place[0] % 2
        columns = pl.ds(aligned((core * HALF + first) * GROUP * WIDTH), heads * GROUP * WIDTH)
        loads = query_loads(queries, partner_queries, query_ref, place, first, heads, tokens, load_sem)
        for n, piece in enumerate(pieces):
            row = aligned((2 * (n // 2) + (core if n % 2 == 0 else 1 - core)) * tokens)
            loads.append(pltpu.make_async_copy(piece, pair_ref.at[pl.ds(row, tokens)], load_sem))

        def states(block):
            here = pl.ds(aligned(block * BLOCK), BLOCK)
            return [
                pltpu.make_async_copy(source.at[:, :, here], target.at[:, :, here], state_sem.at[block])
                for source, target in zip(state_in, state_refs)
            ]

        def store(block):
            here = pl.ds(aligned(block * BLOCK), BLOCK)
            own = block // (blocks // 2) == core
            to = pl.ds(aligned(block % (blocks // 2) * BLOCK), BLOCK)
            mine = pltpu.make_async_copy(done_ref.at[here], out.at[to, columns], store_sem)
            other = pltpu.make_async_copy(done_ref.at[here], out_partner.at[to], store_sem)
            return own, mine, other

        for copy in loads:
            copy.start()
        for block in range(blocks):
            for copy in states(block):
                copy.start()
        for copy in loads:
            copy.wait()

        def before(h, heads_of, here):
            rows = (heads_of.stop - heads_of.start) * BLOCK
            return None if whole else [ref[h, heads_of, here, :].reshape(rows, WIDTH) for ref in state_refs]

        def after(h, at, count, here, top, mixed, total, past):
            if not whole:
                factor = jnp.exp2(past[1] - top)
                mixed, total = past[0] * factor + mixed, total + factor
            done = (mixed / total).astype(jnp.bfloat16)
            for a in range(count):
                done_ref[here, pl.ds((h * GROUP + at + a) * WIDTH, WIDTH)] = done[a * BLOCK : (a + 1) * BLOCK]

        def one_block(block, carry):
            for copy in states(block):
                copy.wait()
            low = document_start(doc_blocks, docs, chip * blocks + block) - (chip - 2) * blocks
            end = 2 * blocks + block + 1 if whole else 2 * blocks
            count = end - low
            least = 0
            for width in (3, 6, 9, LONGEST if whole else LONGEST - 1):
                @pl.when((count <= width) & (count > least))
                def _():
                    start = end - width
                    attend_block(width, heads, query_ref, pair_ref, block, start * BLOCK, start, low, whole,
                                 before, after)
                least = width

            if not whole:
                @pl.when(count <= 0)
                def _():
                    here = pl.ds(aligned(block * BLOCK), BLOCK)
                    for h in range(heads):
                        for a in range(GROUP):
                            done_ref[here, pl.ds((h * GROUP + a) * WIDTH, WIDTH)] = (
                                state_refs[0][h, a, here, :].astype(jnp.bfloat16))

            own, mine, other = store(block)

            @pl.when(own)
            def _():
                mine.start()

            @pl.when(jnp.logical_not(own))
            def _():
                other.start()

            return carry

        lax.fori_loop(0, blocks, one_block, 0)

        def finish(block, carry):
            own, mine, other = store(block)

            @pl.when(own)
            def _():
                mine.wait()

            @pl.when(jnp.logical_not(own))
            def _():
                other.wait()

            return carry

        lax.fori_loop(0, blocks, finish, 0)

    state = (heads, GROUP, 2 * tokens, WIDTH)
    return pl.pallas_call(
        kernel,
        out_shape=(
            jax.ShapeDtypeStruct((tokens, KEY_HEADS * GROUP * WIDTH), jnp.bfloat16),
            jax.ShapeDtypeStruct((tokens, heads * GROUP * WIDTH), jnp.bfloat16),
        ),
        in_specs=[SCALAR, SCALAR, HBM, HBM] + [ANY] * (states_in + 2 * slots + carried),
        out_specs=(ANY, ANY),
        scratch_shapes=[
            pltpu.VMEM((2 * tokens, heads * GROUP * WIDTH), jnp.bfloat16),
            pltpu.VMEM((2 * slots * tokens, 2 * heads * WIDTH), jnp.bfloat16),
            pltpu.VMEM((2 * tokens, heads * GROUP * WIDTH), jnp.bfloat16),
            pltpu.SemaphoreType.DMA(()),
            pltpu.SemaphoreType.DMA(()),
        ] + [pltpu.VMEM(state, jnp.float32)] * states_in + [pltpu.SemaphoreType.DMA((blocks,))],
        input_output_aliases={4 + states_in + 2 * slots: 0} if carried else {},
        compiler_params=pltpu.CompilerParams(vmem_limit_bytes=28 << 20),
        cost_estimate=pl.CostEstimate(flops=heads * 4_000_000_000, transcendentals=0, bytes_accessed=8_000_000),
    )


def last_call(tokens, heads):
    width = heads * GROUP * WIDTH

    def kernel(place, out_in, *rest):
        *returned, out, sem = rest
        copies = []
        for part, source in enumerate(returned):
            other = aligned(((1 - place[0] % 2) * HALF + part * heads) * GROUP * WIDTH)
            copies.append(pltpu.make_async_copy(source, out.at[:, pl.ds(other, width)], sem.at[part]))
            copies[part].start()
        for copy in copies:
            copy.wait()

    return pl.pallas_call(
        kernel,
        out_shape=jax.ShapeDtypeStruct((tokens, KEY_HEADS * GROUP * WIDTH), jnp.bfloat16),
        in_specs=[SCALAR, ANY] + [pl.BlockSpec(memory_space=pltpu.VMEM)] * (HALF // heads),
        out_specs=ANY,
        scratch_shapes=[pltpu.SemaphoreType.DMA((HALF // heads,))],
        input_output_aliases={1: 0},
        compiler_params=pltpu.CompilerParams(vmem_limit_bytes=8 << 20),
    )


def on_device(queries, keys, values, doc_blocks):
    tokens = queries.shape[0]
    docs = doc_blocks.shape[0]
    place = lax.axis_index("ctx").astype(jnp.int32)
    odd = (place // 2) % 2 == 1
    place = place.reshape(1)
    swap = lambda x: permuted(x, lambda i: i ^ 1)
    hop = lambda x: permuted(x, lambda i: i + 4)
    across = lambda x: permuted(x, lambda i: i ^ 2)

    other, own, other_late, own_late = pack_call(tokens, 2)(place, keys, values)
    received = swap(other)
    other_late, received = lax.optimization_barrier((other_late, received))
    received_late = swap(other_late)
    queries, received = lax.optimization_barrier((queries, received))
    partner_queries = swap(queries)
    near = [own, received, own_late, received_late]
    common = (place, doc_blocks, queries, partner_queries)
    relay = lambda n: across(jnp.where(odd, far[n], near[n]))
    far = [hop(x) for x in near[:2]]
    before = [relay(0)]
    late = near[2]
    far.append(hop(late))
    before.append(relay(1))
    last, before[0], far[2] = lax.optimization_barrier((near[3], before[0], far[2]))
    before.append(relay(2))
    far.append(hop(last))
    before.append(permuted(last, lambda i: i + 2))
    before[1], far[2] = lax.optimization_barrier((before[1], far[2]))
    out, partner = far_call(0, 2, tokens, docs, True, False)(*common, *far[:2], *before[:2], *near[:2])
    out, partner_late = far_call(2, 2, tokens, docs, True, True)(*common, *far[2:], *before[2:], *near[2:], out)
    return last_call(tokens, 2)(place, out, swap(partner), swap(partner_late))


def solution(mesh):
    placed = (
        P(("groups", "ctx"), None),
        P(("groups", "ctx"), None),
        P(("groups", "ctx"), None),
        P("groups"),
    )
    return jax.shard_map(
        on_device, mesh=mesh, in_specs=placed, out_specs=P(("groups", "ctx"), None), check_vma=False
    )
```

```python
import math

import jax
import jax.numpy as jnp
from jax import lax
from jax.experimental import pallas as pl
from jax.experimental.pallas import tpu as pltpu
from jax.sharding import PartitionSpec as P

GROUP = 4
WIDTH = 128
KEY_HEADS = 8
HALF = KEY_HEADS // 2
BLOCK = 128
LONGEST = 12
LOG2_SCALE = math.log2(math.e) / math.sqrt(WIDTH)
BLANK = -1e30
ANY = pl.BlockSpec(memory_space=pl.ANY)
HBM = pl.BlockSpec(memory_space=pltpu.HBM)
SCALAR = pl.BlockSpec(memory_space=pltpu.SMEM)


def permuted(array, target):
    devices = lax.axis_size("ctx")
    pairs = [(i, target(i)) for i in range(devices) if 0 <= target(i) < devices]
    return lax.ppermute(array, "ctx", pairs)


def aligned(x):
    return pl.multiple_of(x, 128)


def scores_of(query, key, first, low, diagonal):
    rows = query.shape[0]
    width = key.shape[0] // BLOCK
    scores = lax.dot_general(query, key, (((1,), (1,)), ((), ())), preferred_element_type=jnp.float32)
    tiles = []
    for t in range(width):
        tile = scores[:, t * BLOCK : (t + 1) * BLOCK]
        if diagonal and t == width - 1:
            row = lax.broadcasted_iota(jnp.int32, (rows, BLOCK), 0) & (BLOCK - 1)
            column = lax.broadcasted_iota(jnp.int32, (rows, BLOCK), 1)
            tile = jnp.where(column <= row, tile, BLANK)
        elif t < 2:
            tile = jnp.where(jnp.broadcast_to(first + t >= low, (rows, BLOCK)), tile, BLANK)
        tiles.append(tile)
    return tiles


def attend_block(width, heads, query_ref, pair_ref, block, row, first, low, diagonal, before, after):
    parts = 2
    count = GROUP // parts
    rows = count * BLOCK
    here = pl.ds(aligned(block * BLOCK), BLOCK)
    span = pl.ds(aligned(row), width * BLOCK)
    units = [(h, p) for p in range(parts) for h in range(heads)]

    def score(h, p):
        query = jnp.concatenate(
            [query_ref[here, pl.ds((h * GROUP + p * count + a) * WIDTH, WIDTH)] for a in range(count)], axis=0)
        return scores_of(query, pair_ref[span, pl.ds(h * WIDTH, WIDTH)], first, low, diagonal)

    def weigh(tiles, past):
        top = tiles[0]
        for tile in tiles[1:]:
            top = jnp.maximum(top, tile)
        top = jnp.broadcast_to(jnp.max(top, axis=1, keepdims=True), (rows, BLOCK)) * LOG2_SCALE
        if past is not None:
            top = jnp.maximum(top, past)
        weights = [jnp.exp2(tile * LOG2_SCALE - top).astype(jnp.bfloat16) for tile in tiles]
        return jnp.concatenate(weights, axis=1), top

    def mix(h, weights):
        value = pair_ref[span, pl.ds((heads + h) * WIDTH, WIDTH)]
        value = jnp.concatenate([value, jnp.ones((width * BLOCK, WIDTH), jnp.bfloat16)], axis=1)
        mixed = lax.dot_general(weights, value, (((1,), (0,)), ((), ())), preferred_element_type=jnp.float32)
        return mixed[:, :WIDTH], mixed[:, WIDTH:]

    tiles = [score(*unit) for unit in units]
    past = [before(h, slice(p * count, (p + 1) * count), here) for h, p in units]
    weighed = [weigh(t, None if b is None else b[1]) for t, b in zip(tiles, past)]
    for (h, p), (weights, top), b in zip(units, weighed, past):
        after(h, p * count, count, here, top, *mix(h, weights), b)


def document_start(doc_blocks, docs, here):
    def document(j, state):
        end, begin = state
        end = end + doc_blocks[j]
        return end, jnp.where(end <= here, end, begin)

    return lax.fori_loop(0, docs, document, (jnp.int32(0), jnp.int32(0)))[1]


def pack_call(tokens, heads):
    count = HALF // heads

    def kernel(place, keys, values, *rest):
        targets, buffer, load_sem, store_sem = rest[: 2 * count], *rest[2 * count :]
        core = place[0] % 2
        loads, stores = [], []
        for part in range(count):
            for o in range(2):
                half = core if o == 1 else 1 - core
                for s, source in enumerate((keys, values)):
                    column = aligned((half * HALF + part * heads) * WIDTH)
                    to = pl.ds(s * heads * WIDTH, heads * WIDTH)
                    n = part * 2 + o
                    loads.append(pltpu.make_async_copy(
                        source.at[:, pl.ds(column, heads * WIDTH)], buffer.at[n, :, to], load_sem.at[n]))
                stores.append(pltpu.make_async_copy(buffer.at[n], targets[n], store_sem))
        for copy in loads:
            copy.start()
        for n, copy in enumerate(stores):
            loads[2 * n].wait()
            loads[2 * n + 1].wait()
            copy.start()
        for copy in stores:
            copy.wait()

    shape = jax.ShapeDtypeStruct((tokens, 2 * heads * WIDTH), jnp.bfloat16)
    return pl.pallas_call(
        kernel,
        out_shape=[shape] * (2 * count),
        in_specs=[SCALAR, HBM, HBM],
        out_specs=[HBM] * (2 * count),
        scratch_shapes=[
            pltpu.VMEM((2 * count, tokens, 2 * heads * WIDTH), jnp.bfloat16),
            pltpu.SemaphoreType.DMA((2 * count,)),
            pltpu.SemaphoreType.DMA(()),
        ],
    )


def query_loads(queries, partner_queries, query_ref, place, first, heads, tokens, sem):
    core = place[0] % 2
    columns = pl.ds(aligned((core * HALF + first) * GROUP * WIDTH), heads * GROUP * WIDTH)
    return [
        pltpu.make_async_copy(
            source.at[:, columns], query_ref.at[pl.ds(aligned((core if side == 0 else 1 - core) * tokens), tokens)], sem)
        for side, source in enumerate((queries, partner_queries))
    ]


def near_call(first, heads, tokens, docs):
    blocks = 2 * tokens // BLOCK
    pad = 2 * BLOCK

    def kernel(place, doc_blocks, queries, partner_queries, own, received, mix_out, log_out,
               query_ref, pair_ref, mix_ref, log_ref, load_sem, store_sem):
        chip = place[0] // 2
        core = place[0] % 2
        loads = query_loads(queries, partner_queries, query_ref, place, first, heads, tokens, load_sem)
        for side, piece in enumerate((own, received)):
            row = aligned(pad + (core if side == 0 else 1 - core) * tokens)
            loads.append(pltpu.make_async_copy(piece, pair_ref.at[pl.ds(row, tokens)], load_sem))
        for copy in loads:
            copy.start()
        pair_ref[:pad, :] = jnp.zeros((pad, 2 * heads * WIDTH), jnp.bfloat16)
        for copy in loads:
            copy.wait()

        def stores(block):
            here = pl.ds(aligned(block * BLOCK), BLOCK)
            return [
                pltpu.make_async_copy(mix_ref.at[:, :, here], mix_out.at[:, :, here], store_sem),
                pltpu.make_async_copy(log_ref.at[:, :, here], log_out.at[:, :, here], store_sem),
            ]

        def before(h, heads_of, here):
            return None

        def after(h, at, count, here, top, mixed, total, past):
            mix_ref[h, at : at + count, here, :] = (mixed / total).reshape(count, BLOCK, WIDTH)
            log_ref[h, at : at + count, here, :] = (top + jnp.log2(total)).reshape(count, BLOCK, WIDTH)

        def one_block(block, carry):
            here = chip * blocks + block
            low = jnp.maximum(document_start(doc_blocks, docs, here) - chip * blocks, 0)
            count = block - low + 1
            for width in range(3, blocks + 1, 3):
                @pl.when((count <= width) & (count > width - 3))
                def _():
                    start = block - width + 1
                    attend_block(width, heads, query_ref, pair_ref, block, pad + start * BLOCK, start, low, True,
                                 before, after)
            for copy in stores(block):
                copy.start()
            return carry

        lax.fori_loop(0, blocks, one_block, 0)

        def finish(block, carry):
            for copy in stores(block):
                copy.wait()
            return carry

        lax.fori_loop(0, blocks, finish, 0)

    state = jax.ShapeDtypeStruct((heads, GROUP, 2 * tokens, WIDTH), jnp.float32)
    return pl.pallas_call(
        kernel,
        out_shape=(state, state),
        in_specs=[SCALAR, SCALAR] + [HBM] * 4,
        out_specs=(ANY, ANY),
        scratch_shapes=[
            pltpu.VMEM((2 * tokens, heads * GROUP * WIDTH), jnp.bfloat16),
            pltpu.VMEM((pad + 2 * tokens, 2 * heads * WIDTH), jnp.bfloat16),
            pltpu.VMEM(state.shape, jnp.float32),
            pltpu.VMEM(state.shape, jnp.float32),
            pltpu.SemaphoreType.DMA(()),
            pltpu.SemaphoreType.DMA(()),
        ],
        compiler_params=pltpu.CompilerParams(vmem_limit_bytes=20 << 20),
        cost_estimate=pl.CostEstimate(flops=heads * 3_000_000_000, transcendentals=0, bytes_accessed=8_000_000),
    )


def far_call(first, heads, tokens, docs, whole, carried):
    blocks = 2 * tokens // BLOCK
    slots = 3 if whole else 2
    states_in = 0 if whole else 2

    def kernel(place, doc_blocks, queries, partner_queries, *rest):
        state_in, rest = rest[:states_in], rest[states_in:]
        pieces, rest = rest[: 2 * slots], rest[2 * slots + carried :]
        out, out_partner, query_ref, pair_ref, done_ref, load_sem, store_sem, *rest = rest
        state_refs, state_sem = rest[:states_in], rest[-1]
        chip = place[0] // 2
        core = place[0] % 2
        columns = pl.ds(aligned((core * HALF + first) * GROUP * WIDTH), heads * GROUP * WIDTH)
        loads = query_loads(queries, partner_queries, query_ref, place, first, heads, tokens, load_sem)
        for n, piece in enumerate(pieces):
            row = aligned((2 * (n // 2) + (core if n % 2 == 0 else 1 - core)) * tokens)
            loads.append(pltpu.make_async_copy(piece, pair_ref.at[pl.ds(row, tokens)], load_sem))

        def states(block):
            here = pl.ds(aligned(block * BLOCK), BLOCK)
            return [
                pltpu.make_async_copy(source.at[:, :, here], target.at[:, :, here], state_sem.at[block])
                for source, target in zip(state_in, state_refs)
            ]

        def store(block):
            here = pl.ds(aligned(block * BLOCK), BLOCK)
            own = block // (blocks // 2) == core
            to = pl.ds(aligned(block % (blocks // 2) * BLOCK), BLOCK)
            mine = pltpu.make_async_copy(done_ref.at[here], out.at[to, columns], store_sem)
            other = pltpu.make_async_copy(done_ref.at[here], out_partner.at[to], store_sem)
            return own, mine, other

        for copy in loads:
            copy.start()
        for block in range(blocks):
            for copy in states(block):
                copy.start()
        for copy in loads:
            copy.wait()

        def before(h, heads_of, here):
            rows = (heads_of.stop - heads_of.start) * BLOCK
            return None if whole else [ref[h, heads_of, here, :].reshape(rows, WIDTH) for ref in state_refs]

        def after(h, at, count, here, top, mixed, total, past):
            if not whole:
                factor = jnp.exp2(past[1] - top)
                mixed, total = past[0] * factor + mixed, total + factor
            done = (mixed / total).astype(jnp.bfloat16)
            for a in range(count):
                done_ref[here, pl.ds((h * GROUP + at + a) * WIDTH, WIDTH)] = done[a * BLOCK : (a + 1) * BLOCK]

        def one_block(block, carry):
            for copy in states(block):
                copy.wait()
            low = document_start(doc_blocks, docs, chip * blocks + block) - (chip - 2) * blocks
            end = 2 * blocks + block + 1 if whole else 2 * blocks
            count = end - low
            least = 0
            for width in (3, 6, 9, LONGEST if whole else LONGEST - 1):
                @pl.when((count <= width) & (count > least))
                def _():
                    start = end - width
                    attend_block(width, heads, query_ref, pair_ref, block, start * BLOCK, start, low, whole,
                                 before, after)
                least = width

            if not whole:
                @pl.when(count <= 0)
                def _():
                    here = pl.ds(aligned(block * BLOCK), BLOCK)
                    for h in range(heads):
                        for a in range(GROUP):
                            done_ref[here, pl.ds((h * GROUP + a) * WIDTH, WIDTH)] = (
                                state_refs[0][h, a, here, :].astype(jnp.bfloat16))

            own, mine, other = store(block)

            @pl.when(own)
            def _():
                mine.start()

            @pl.when(jnp.logical_not(own))
            def _():
                other.start()

            return carry

        lax.fori_loop(0, blocks, one_block, 0)

        def finish(block, carry):
            own, mine, other = store(block)

            @pl.when(own)
            def _():
                mine.wait()

            @pl.when(jnp.logical_not(own))
            def _():
                other.wait()

            return carry

        lax.fori_loop(0, blocks, finish, 0)

    state = (heads, GROUP, 2 * tokens, WIDTH)
    return pl.pallas_call(
        kernel,
        out_shape=(
            jax.ShapeDtypeStruct((tokens, KEY_HEADS * GROUP * WIDTH), jnp.bfloat16),
            jax.ShapeDtypeStruct((tokens, heads * GROUP * WIDTH), jnp.bfloat16),
        ),
        in_specs=[SCALAR, SCALAR, HBM, HBM] + [ANY] * (states_in + 2 * slots + carried),
        out_specs=(ANY, ANY),
        scratch_shapes=[
            pltpu.VMEM((2 * tokens, heads * GROUP * WIDTH), jnp.bfloat16),
            pltpu.VMEM((2 * slots * tokens, 2 * heads * WIDTH), jnp.bfloat16),
            pltpu.VMEM((2 * tokens, heads * GROUP * WIDTH), jnp.bfloat16),
            pltpu.SemaphoreType.DMA(()),
            pltpu.SemaphoreType.DMA(()),
        ] + [pltpu.VMEM(state, jnp.float32)] * states_in + [pltpu.SemaphoreType.DMA((blocks,))],
        input_output_aliases={4 + states_in + 2 * slots: 0} if carried else {},
        compiler_params=pltpu.CompilerParams(vmem_limit_bytes=28 << 20),
        cost_estimate=pl.CostEstimate(flops=heads * 4_000_000_000, transcendentals=0, bytes_accessed=8_000_000),
    )


def last_call(tokens, heads):
    width = heads * GROUP * WIDTH

    def kernel(place, out_in, *rest):
        *returned, out, sem = rest
        copies = []
        for part, source in enumerate(returned):
            other = aligned(((1 - place[0] % 2) * HALF + part * heads) * GROUP * WIDTH)
            copies.append(pltpu.make_async_copy(source, out.at[:, pl.ds(other, width)], sem.at[part]))
            copies[part].start()
        for copy in copies:
            copy.wait()

    return pl.pallas_call(
        kernel,
        out_shape=jax.ShapeDtypeStruct((tokens, KEY_HEADS * GROUP * WIDTH), jnp.bfloat16),
        in_specs=[SCALAR, ANY] + [pl.BlockSpec(memory_space=pltpu.VMEM)] * (HALF // heads),
        out_specs=ANY,
        scratch_shapes=[pltpu.SemaphoreType.DMA((HALF // heads,))],
        input_output_aliases={1: 0},
        compiler_params=pltpu.CompilerParams(vmem_limit_bytes=8 << 20),
    )


def on_device(queries, keys, values, doc_blocks):
    tokens = queries.shape[0]
    docs = doc_blocks.shape[0]
    place = lax.axis_index("ctx").astype(jnp.int32)
    odd = (place // 2) % 2 == 1
    place = place.reshape(1)
    swap = lambda x: permuted(x, lambda i: i ^ 1)
    hop = lambda x: permuted(x, lambda i: i + 4)
    across = lambda x: permuted(x, lambda i: i ^ 2)

    other, own, other_late, own_late = pack_call(tokens, 2)(place, keys, values)
    received = swap(other)
    other_late, received = lax.optimization_barrier((other_late, received))
    received_late = swap(other_late)
    queries, received = lax.optimization_barrier((queries, received))
    partner_queries = swap(queries)
    near = [own, received, own_late, received_late]
    common = (place, doc_blocks, queries, partner_queries)
    relay = lambda n: across(jnp.where(odd, far[n], near[n]))
    far = [hop(x) for x in near[:2]]
    before = [relay(0)]
    late = near[2]
    far.append(hop(late))
    before.append(relay(1))
    last, far[1] = lax.optimization_barrier((near[3], far[1]))
    final, before[0] = lax.optimization_barrier((near[3], before[0]))
    before[0], far[2] = lax.optimization_barrier((before[0], far[2]))
    before.append(relay(2))
    far.append(hop(last))
    before.append(permuted(final, lambda i: i + 2))
    before[1], far[2] = lax.optimization_barrier((before[1], far[2]))
    out, partner = far_call(0, 2, tokens, docs, True, False)(*common, *far[:2], *before[:2], *near[:2])
    out, partner_late = far_call(2, 2, tokens, docs, True, True)(*common, *far[2:], *before[2:], *near[2:], out)
    return last_call(tokens, 2)(place, out, swap(partner), swap(partner_late))


def solution(mesh):
    placed = (
        P(("groups", "ctx"), None),
        P(("groups", "ctx"), None),
        P(("groups", "ctx"), None),
        P("groups"),
    )
    return jax.shard_map(
        on_device, mesh=mesh, in_specs=placed, out_specs=P(("groups", "ctx"), None), check_vma=False
    )
```

```python
import math

import jax
import jax.numpy as jnp
from jax import lax
from jax.experimental import pallas as pl
from jax.experimental.pallas import tpu as pltpu
from jax.sharding import PartitionSpec as P

GROUP = 4
WIDTH = 128
KEY_HEADS = 8
HALF = KEY_HEADS // 2
BLOCK = 128
LONGEST = 12
LOG2_SCALE = math.log2(math.e) / math.sqrt(WIDTH)
BLANK = -1e30
ANY = pl.BlockSpec(memory_space=pl.ANY)
HBM = pl.BlockSpec(memory_space=pltpu.HBM)
SCALAR = pl.BlockSpec(memory_space=pltpu.SMEM)


def permuted(array, target):
    devices = lax.axis_size("ctx")
    pairs = [(i, target(i)) for i in range(devices) if 0 <= target(i) < devices]
    return lax.ppermute(array, "ctx", pairs)


def aligned(x):
    return pl.multiple_of(x, 128)


def scores_of(query, key, first, low, diagonal):
    rows = query.shape[0]
    width = key.shape[0] // BLOCK
    scores = lax.dot_general(query, key, (((1,), (1,)), ((), ())), preferred_element_type=jnp.float32)
    tiles = []
    for t in range(width):
        tile = scores[:, t * BLOCK : (t + 1) * BLOCK]
        if diagonal and t == width - 1:
            row = lax.broadcasted_iota(jnp.int32, (rows, BLOCK), 0) & (BLOCK - 1)
            column = lax.broadcasted_iota(jnp.int32, (rows, BLOCK), 1)
            tile = jnp.where(column <= row, tile, BLANK)
        elif t < 2:
            tile = jnp.where(jnp.broadcast_to(first + t >= low, (rows, BLOCK)), tile, BLANK)
        tiles.append(tile)
    return tiles


def attend_block(width, heads, query_ref, pair_ref, block, row, first, low, diagonal, before, after):
    parts = 2
    count = GROUP // parts
    rows = count * BLOCK
    here = pl.ds(aligned(block * BLOCK), BLOCK)
    span = pl.ds(aligned(row), width * BLOCK)
    units = [(h, p) for p in range(parts) for h in range(heads)]

    def score(h, p):
        query = jnp.concatenate(
            [query_ref[here, pl.ds((h * GROUP + p * count + a) * WIDTH, WIDTH)] for a in range(count)], axis=0)
        return scores_of(query, pair_ref[span, pl.ds(h * WIDTH, WIDTH)], first, low, diagonal)

    def weigh(tiles, past):
        top = tiles[0]
        for tile in tiles[1:]:
            top = jnp.maximum(top, tile)
        top = jnp.broadcast_to(jnp.max(top, axis=1, keepdims=True), (rows, BLOCK)) * LOG2_SCALE
        if past is not None:
            top = jnp.maximum(top, past)
        weights = [jnp.exp2(tile * LOG2_SCALE - top).astype(jnp.bfloat16) for tile in tiles]
        return jnp.concatenate(weights, axis=1), top

    def mix(h, weights):
        value = pair_ref[span, pl.ds((heads + h) * WIDTH, WIDTH)]
        value = jnp.concatenate([value, jnp.ones((width * BLOCK, WIDTH), jnp.bfloat16)], axis=1)
        mixed = lax.dot_general(weights, value, (((1,), (0,)), ((), ())), preferred_element_type=jnp.float32)
        return mixed[:, :WIDTH], mixed[:, WIDTH:]

    tiles = [score(*unit) for unit in units]
    past = [before(h, slice(p * count, (p + 1) * count), here) for h, p in units]
    weighed = [weigh(t, None if b is None else b[1]) for t, b in zip(tiles, past)]
    for (h, p), (weights, top), b in zip(units, weighed, past):
        after(h, p * count, count, here, top, *mix(h, weights), b)


def document_start(doc_blocks, docs, here):
    def document(j, state):
        end, begin = state
        end = end + doc_blocks[j]
        return end, jnp.where(end <= here, end, begin)

    return lax.fori_loop(0, docs, document, (jnp.int32(0), jnp.int32(0)))[1]


def pack_call(tokens, heads):
    count = HALF // heads

    def kernel(place, keys, values, *rest):
        targets, buffer, load_sem, store_sem = rest[: 2 * count], *rest[2 * count :]
        core = place[0] % 2
        loads, stores = [], []
        for part in range(count):
            for o in range(2):
                half = core if o == 1 else 1 - core
                for s, source in enumerate((keys, values)):
                    column = aligned((half * HALF + part * heads) * WIDTH)
                    to = pl.ds(s * heads * WIDTH, heads * WIDTH)
                    n = part * 2 + o
                    loads.append(pltpu.make_async_copy(
                        source.at[:, pl.ds(column, heads * WIDTH)], buffer.at[n, :, to], load_sem.at[n]))
                stores.append(pltpu.make_async_copy(buffer.at[n], targets[n], store_sem))
        for copy in loads:
            copy.start()
        for n, copy in enumerate(stores):
            loads[2 * n].wait()
            loads[2 * n + 1].wait()
            copy.start()
        for copy in stores:
            copy.wait()

    shape = jax.ShapeDtypeStruct((tokens, 2 * heads * WIDTH), jnp.bfloat16)
    return pl.pallas_call(
        kernel,
        out_shape=[shape] * (2 * count),
        in_specs=[SCALAR, HBM, HBM],
        out_specs=[HBM] * (2 * count),
        scratch_shapes=[
            pltpu.VMEM((2 * count, tokens, 2 * heads * WIDTH), jnp.bfloat16),
            pltpu.SemaphoreType.DMA((2 * count,)),
            pltpu.SemaphoreType.DMA(()),
        ],
    )


def query_loads(queries, partner_queries, query_ref, place, first, heads, tokens, sem):
    core = place[0] % 2
    columns = pl.ds(aligned((core * HALF + first) * GROUP * WIDTH), heads * GROUP * WIDTH)
    return [
        pltpu.make_async_copy(
            source.at[:, columns], query_ref.at[pl.ds(aligned((core if side == 0 else 1 - core) * tokens), tokens)], sem)
        for side, source in enumerate((queries, partner_queries))
    ]


def near_call(first, heads, tokens, docs):
    blocks = 2 * tokens // BLOCK
    pad = 2 * BLOCK

    def kernel(place, doc_blocks, queries, partner_queries, own, received, mix_out, log_out,
               query_ref, pair_ref, mix_ref, log_ref, load_sem, store_sem):
        chip = place[0] // 2
        core = place[0] % 2
        loads = query_loads(queries, partner_queries, query_ref, place, first, heads, tokens, load_sem)
        for side, piece in enumerate((own, received)):
            row = aligned(pad + (core if side == 0 else 1 - core) * tokens)
            loads.append(pltpu.make_async_copy(piece, pair_ref.at[pl.ds(row, tokens)], load_sem))
        for copy in loads:
            copy.start()
        pair_ref[:pad, :] = jnp.zeros((pad, 2 * heads * WIDTH), jnp.bfloat16)
        for copy in loads:
            copy.wait()

        def stores(block):
            here = pl.ds(aligned(block * BLOCK), BLOCK)
            return [
                pltpu.make_async_copy(mix_ref.at[:, :, here], mix_out.at[:, :, here], store_sem),
                pltpu.make_async_copy(log_ref.at[:, :, here], log_out.at[:, :, here], store_sem),
            ]

        def before(h, heads_of, here):
            return None

        def after(h, at, count, here, top, mixed, total, past):
            mix_ref[h, at : at + count, here, :] = (mixed / total).reshape(count, BLOCK, WIDTH)
            log_ref[h, at : at + count, here, :] = (top + jnp.log2(total)).reshape(count, BLOCK, WIDTH)

        def one_block(block, carry):
            here = chip * blocks + block
            low = jnp.maximum(document_start(doc_blocks, docs, here) - chip * blocks, 0)
            count = block - low + 1
            for width in range(3, blocks + 1, 3):
                @pl.when((count <= width) & (count > width - 3))
                def _():
                    start = block - width + 1
                    attend_block(width, heads, query_ref, pair_ref, block, pad + start * BLOCK, start, low, True,
                                 before, after)
            for copy in stores(block):
                copy.start()
            return carry

        lax.fori_loop(0, blocks, one_block, 0)

        def finish(block, carry):
            for copy in stores(block):
                copy.wait()
            return carry

        lax.fori_loop(0, blocks, finish, 0)

    state = jax.ShapeDtypeStruct((heads, GROUP, 2 * tokens, WIDTH), jnp.float32)
    return pl.pallas_call(
        kernel,
        out_shape=(state, state),
        in_specs=[SCALAR, SCALAR] + [HBM] * 4,
        out_specs=(ANY, ANY),
        scratch_shapes=[
            pltpu.VMEM((2 * tokens, heads * GROUP * WIDTH), jnp.bfloat16),
            pltpu.VMEM((pad + 2 * tokens, 2 * heads * WIDTH), jnp.bfloat16),
            pltpu.VMEM(state.shape, jnp.float32),
            pltpu.VMEM(state.shape, jnp.float32),
            pltpu.SemaphoreType.DMA(()),
            pltpu.SemaphoreType.DMA(()),
        ],
        compiler_params=pltpu.CompilerParams(vmem_limit_bytes=20 << 20),
        cost_estimate=pl.CostEstimate(flops=heads * 3_000_000_000, transcendentals=0, bytes_accessed=8_000_000),
    )


def far_call(first, heads, tokens, docs, whole, carried):
    blocks = 2 * tokens // BLOCK
    slots = 3 if whole else 2
    states_in = 0 if whole else 2

    def kernel(place, doc_blocks, queries, partner_queries, *rest):
        state_in, rest = rest[:states_in], rest[states_in:]
        pieces, rest = rest[: 2 * slots], rest[2 * slots + carried :]
        out, out_partner, query_ref, pair_ref, done_ref, load_sem, store_sem, *rest = rest
        state_refs, state_sem = rest[:states_in], rest[-1]
        chip = place[0] // 2
        core = place[0] % 2
        columns = pl.ds(aligned((core * HALF + first) * GROUP * WIDTH), heads * GROUP * WIDTH)
        loads = query_loads(queries, partner_queries, query_ref, place, first, heads, tokens, load_sem)
        for n, piece in enumerate(pieces):
            row = aligned((2 * (n // 2) + (core if n % 2 == 0 else 1 - core)) * tokens)
            loads.append(pltpu.make_async_copy(piece, pair_ref.at[pl.ds(row, tokens)], load_sem))

        def states(block):
            here = pl.ds(aligned(block * BLOCK), BLOCK)
            return [
                pltpu.make_async_copy(source.at[:, :, here], target.at[:, :, here], state_sem.at[block])
                for source, target in zip(state_in, state_refs)
            ]

        def store(block):
            here = pl.ds(aligned(block * BLOCK), BLOCK)
            own = block // (blocks // 2) == core
            to = pl.ds(aligned(block % (blocks // 2) * BLOCK), BLOCK)
            mine = pltpu.make_async_copy(done_ref.at[here], out.at[to, columns], store_sem)
            other = pltpu.make_async_copy(done_ref.at[here], out_partner.at[to], store_sem)
            return own, mine, other

        for copy in loads:
            copy.start()
        for block in range(blocks):
            for copy in states(block):
                copy.start()
        for copy in loads:
            copy.wait()

        def before(h, heads_of, here):
            rows = (heads_of.stop - heads_of.start) * BLOCK
            return None if whole else [ref[h, heads_of, here, :].reshape(rows, WIDTH) for ref in state_refs]

        def after(h, at, count, here, top, mixed, total, past):
            if not whole:
                factor = jnp.exp2(past[1] - top)
                mixed, total = past[0] * factor + mixed, total + factor
            done = (mixed / total).astype(jnp.bfloat16)
            for a in range(count):
                done_ref[here, pl.ds((h * GROUP + at + a) * WIDTH, WIDTH)] = done[a * BLOCK : (a + 1) * BLOCK]

        def one_block(block, carry):
            for copy in states(block):
                copy.wait()
            low = document_start(doc_blocks, docs, chip * blocks + block) - (chip - 2) * blocks
            end = 2 * blocks + block + 1 if whole else 2 * blocks
            count = end - low
            least = 0
            for width in range(2, LONGEST + 1, 2):
                @pl.when((count <= width) & (count > least))
                def _():
                    start = end - width
                    attend_block(width, heads, query_ref, pair_ref, block, start * BLOCK, start, low, whole,
                                 before, after)
                least = width

            if not whole:
                @pl.when(count <= 0)
                def _():
                    here = pl.ds(aligned(block * BLOCK), BLOCK)
                    for h in range(heads):
                        for a in range(GROUP):
                            done_ref[here, pl.ds((h * GROUP + a) * WIDTH, WIDTH)] = (
                                state_refs[0][h, a, here, :].astype(jnp.bfloat16))

            own, mine, other = store(block)

            @pl.when(own)
            def _():
                mine.start()

            @pl.when(jnp.logical_not(own))
            def _():
                other.start()

            return carry

        lax.fori_loop(0, blocks, one_block, 0)

        def finish(block, carry):
            own, mine, other = store(block)

            @pl.when(own)
            def _():
                mine.wait()

            @pl.when(jnp.logical_not(own))
            def _():
                other.wait()

            return carry

        lax.fori_loop(0, blocks, finish, 0)

    state = (heads, GROUP, 2 * tokens, WIDTH)
    return pl.pallas_call(
        kernel,
        out_shape=(
            jax.ShapeDtypeStruct((tokens, KEY_HEADS * GROUP * WIDTH), jnp.bfloat16),
            jax.ShapeDtypeStruct((tokens, heads * GROUP * WIDTH), jnp.bfloat16),
        ),
        in_specs=[SCALAR, SCALAR, HBM, HBM] + [ANY] * (states_in + 2 * slots + carried),
        out_specs=(ANY, ANY),
        scratch_shapes=[
            pltpu.VMEM((2 * tokens, heads * GROUP * WIDTH), jnp.bfloat16),
            pltpu.VMEM((2 * slots * tokens, 2 * heads * WIDTH), jnp.bfloat16),
            pltpu.VMEM((2 * tokens, heads * GROUP * WIDTH), jnp.bfloat16),
            pltpu.SemaphoreType.DMA(()),
            pltpu.SemaphoreType.DMA(()),
        ] + [pltpu.VMEM(state, jnp.float32)] * states_in + [pltpu.SemaphoreType.DMA((blocks,))],
        input_output_aliases={4 + states_in + 2 * slots: 0} if carried else {},
        compiler_params=pltpu.CompilerParams(vmem_limit_bytes=28 << 20),
        cost_estimate=pl.CostEstimate(flops=heads * 4_000_000_000, transcendentals=0, bytes_accessed=8_000_000),
    )


def last_call(tokens, heads):
    width = heads * GROUP * WIDTH

    def kernel(place, out_in, *rest):
        *returned, out, sem = rest
        copies = []
        for part, source in enumerate(returned):
            other = aligned(((1 - place[0] % 2) * HALF + part * heads) * GROUP * WIDTH)
            copies.append(pltpu.make_async_copy(source, out.at[:, pl.ds(other, width)], sem.at[part]))
            copies[part].start()
        for copy in copies:
            copy.wait()

    return pl.pallas_call(
        kernel,
        out_shape=jax.ShapeDtypeStruct((tokens, KEY_HEADS * GROUP * WIDTH), jnp.bfloat16),
        in_specs=[SCALAR, ANY] + [pl.BlockSpec(memory_space=pltpu.VMEM)] * (HALF // heads),
        out_specs=ANY,
        scratch_shapes=[pltpu.SemaphoreType.DMA((HALF // heads,))],
        input_output_aliases={1: 0},
        compiler_params=pltpu.CompilerParams(vmem_limit_bytes=8 << 20),
    )


def on_device(queries, keys, values, doc_blocks):
    tokens = queries.shape[0]
    docs = doc_blocks.shape[0]
    place = lax.axis_index("ctx").astype(jnp.int32)
    odd = (place // 2) % 2 == 1
    place = place.reshape(1)
    swap = lambda x: permuted(x, lambda i: i ^ 1)
    hop = lambda x: permuted(x, lambda i: i + 4)
    across = lambda x: permuted(x, lambda i: i ^ 2)

    other, own, other_late, own_late = pack_call(tokens, 2)(place, keys, values)
    received = swap(other)
    received_late = swap(other_late)
    partner_queries = swap(queries)
    near = [own, received, own_late, received_late]
    common = (place, doc_blocks, queries, partner_queries)
    relay = lambda n: across(jnp.where(odd, far[n], near[n]))
    far = [hop(x) for x in near[:2]]
    before = [relay(0)]
    late = near[2]
    far.append(hop(late))
    before.append(relay(1))
    last, far[1] = lax.optimization_barrier((near[3], far[1]))
    final, before[0] = lax.optimization_barrier((near[3], before[0]))
    before[0], far[2] = lax.optimization_barrier((before[0], far[2]))
    before.append(relay(2))
    far.append(hop(last))
    before.append(permuted(final, lambda i: i + 2))
    before[1], far[2] = lax.optimization_barrier((before[1], far[2]))
    out, partner = far_call(0, 2, tokens, docs, True, False)(*common, *far[:2], *before[:2], *near[:2])
    out, partner_late = far_call(2, 2, tokens, docs, True, True)(*common, *far[2:], *before[2:], *near[2:], out)
    return last_call(tokens, 2)(place, out, swap(partner), swap(partner_late))


def solution(mesh):
    placed = (
        P(("groups", "ctx"), None),
        P(("groups", "ctx"), None),
        P(("groups", "ctx"), None),
        P("groups"),
    )
    return jax.shard_map(
        on_device, mesh=mesh, in_specs=placed, out_specs=P(("groups", "ctx"), None), check_vma=False
    )
```

```python
import math

import jax
import jax.numpy as jnp
from jax import lax
from jax.experimental import pallas as pl
from jax.experimental.pallas import tpu as pltpu
from jax.sharding import PartitionSpec as P

GROUP = 4
WIDTH = 128
KEY_HEADS = 8
HALF = KEY_HEADS // 2
BLOCK = 128
LONGEST = 12
LOG2_SCALE = math.log2(math.e) / math.sqrt(WIDTH)
BLANK = -1e30
ANY = pl.BlockSpec(memory_space=pl.ANY)
HBM = pl.BlockSpec(memory_space=pltpu.HBM)
SCALAR = pl.BlockSpec(memory_space=pltpu.SMEM)


def permuted(array, target):
    devices = lax.axis_size("ctx")
    pairs = [(i, target(i)) for i in range(devices) if 0 <= target(i) < devices]
    return lax.ppermute(array, "ctx", pairs)


def aligned(x):
    return pl.multiple_of(x, 128)


def scores_of(query, key, first, low, diagonal):
    rows = query.shape[0]
    width = key.shape[0] // BLOCK
    scores = lax.dot_general(query, key, (((1,), (1,)), ((), ())), preferred_element_type=jnp.float32)
    tiles = []
    for t in range(width):
        tile = scores[:, t * BLOCK : (t + 1) * BLOCK]
        if diagonal and t == width - 1:
            row = lax.broadcasted_iota(jnp.int32, (rows, BLOCK), 0) & (BLOCK - 1)
            column = lax.broadcasted_iota(jnp.int32, (rows, BLOCK), 1)
            tile = jnp.where(column <= row, tile, BLANK)
        elif t < 1:
            tile = jnp.where(jnp.broadcast_to(first + t >= low, (rows, BLOCK)), tile, BLANK)
        tiles.append(tile)
    return tiles


def attend_block(width, heads, query_ref, pair_ref, block, row, first, low, diagonal, before, after):
    parts = 1
    count = GROUP // parts
    rows = count * BLOCK
    here = pl.ds(aligned(block * BLOCK), BLOCK)
    span = pl.ds(aligned(row), width * BLOCK)
    units = [(h, p) for p in range(parts) for h in range(heads)]

    def score(h, p):
        query = jnp.concatenate(
            [query_ref[here, pl.ds((h * GROUP + p * count + a) * WIDTH, WIDTH)] for a in range(count)], axis=0)
        return scores_of(query, pair_ref[span, pl.ds(h * WIDTH, WIDTH)], first, low, diagonal)

    def weigh(tiles, past):
        top = tiles[0]
        for tile in tiles[1:]:
            top = jnp.maximum(top, tile)
        top = jnp.broadcast_to(jnp.max(top, axis=1, keepdims=True), (rows, BLOCK)) * LOG2_SCALE
        if past is not None:
            top = jnp.maximum(top, past)
        weights = [jnp.exp2(tile * LOG2_SCALE - top).astype(jnp.bfloat16) for tile in tiles]
        return jnp.concatenate(weights, axis=1), top

    def mix(h, weights):
        value = pair_ref[span, pl.ds((heads + h) * WIDTH, WIDTH)]
        value = jnp.concatenate([value, jnp.ones((width * BLOCK, WIDTH), jnp.bfloat16)], axis=1)
        mixed = lax.dot_general(weights, value, (((1,), (0,)), ((), ())), preferred_element_type=jnp.float32)
        return mixed[:, :WIDTH], mixed[:, WIDTH:]

    tiles = [score(*unit) for unit in units]
    past = [before(h, slice(p * count, (p + 1) * count), here) for h, p in units]
    weighed = [weigh(t, None if b is None else b[1]) for t, b in zip(tiles, past)]
    for (h, p), (weights, top), b in zip(units, weighed, past):
        after(h, p * count, count, here, top, *mix(h, weights), b)


def document_start(doc_blocks, docs, here):
    def document(j, state):
        end, begin = state
        end = end + doc_blocks[j]
        return end, jnp.where(end <= here, end, begin)

    return lax.fori_loop(0, docs, document, (jnp.int32(0), jnp.int32(0)))[1]


def pack_call(tokens, heads):
    count = HALF // heads

    def kernel(place, keys, values, *rest):
        targets, buffer, load_sem, store_sem = rest[: 2 * count], *rest[2 * count :]
        core = place[0] % 2
        loads, stores = [], []
        for part in range(count):
            for o in range(2):
                half = core if o == 1 else 1 - core
                for s, source in enumerate((keys, values)):
                    column = aligned((half * HALF + part * heads) * WIDTH)
                    to = pl.ds(s * heads * WIDTH, heads * WIDTH)
                    n = part * 2 + o
                    loads.append(pltpu.make_async_copy(
                        source.at[:, pl.ds(column, heads * WIDTH)], buffer.at[n, :, to], load_sem.at[n]))
                stores.append(pltpu.make_async_copy(buffer.at[n], targets[n], store_sem))
        for copy in loads:
            copy.start()
        for n, copy in enumerate(stores):
            loads[2 * n].wait()
            loads[2 * n + 1].wait()
            copy.start()
        for copy in stores:
            copy.wait()

    shape = jax.ShapeDtypeStruct((tokens, 2 * heads * WIDTH), jnp.bfloat16)
    return pl.pallas_call(
        kernel,
        out_shape=[shape] * (2 * count),
        in_specs=[SCALAR, HBM, HBM],
        out_specs=[HBM] * (2 * count),
        scratch_shapes=[
            pltpu.VMEM((2 * count, tokens, 2 * heads * WIDTH), jnp.bfloat16),
            pltpu.SemaphoreType.DMA((2 * count,)),
            pltpu.SemaphoreType.DMA(()),
        ],
    )


def query_loads(queries, partner_queries, query_ref, place, first, heads, tokens, sem):
    core = place[0] % 2
    columns = pl.ds(aligned((core * HALF + first) * GROUP * WIDTH), heads * GROUP * WIDTH)
    return [
        pltpu.make_async_copy(
            source.at[:, columns], query_ref.at[pl.ds(aligned((core if side == 0 else 1 - core) * tokens), tokens)], sem)
        for side, source in enumerate((queries, partner_queries))
    ]


def near_call(first, heads, tokens, docs):
    blocks = 2 * tokens // BLOCK
    pad = 2 * BLOCK

    def kernel(place, doc_blocks, queries, partner_queries, own, received, mix_out, log_out,
               query_ref, pair_ref, mix_ref, log_ref, load_sem, store_sem):
        chip = place[0] // 2
        core = place[0] % 2
        loads = query_loads(queries, partner_queries, query_ref, place, first, heads, tokens, load_sem)
        for side, piece in enumerate((own, received)):
            row = aligned(pad + (core if side == 0 else 1 - core) * tokens)
            loads.append(pltpu.make_async_copy(piece, pair_ref.at[pl.ds(row, tokens)], load_sem))
        for copy in loads:
            copy.start()
        pair_ref[:pad, :] = jnp.zeros((pad, 2 * heads * WIDTH), jnp.bfloat16)
        for copy in loads:
            copy.wait()

        def stores(block):
            here = pl.ds(aligned(block * BLOCK), BLOCK)
            return [
                pltpu.make_async_copy(mix_ref.at[:, :, here], mix_out.at[:, :, here], store_sem),
                pltpu.make_async_copy(log_ref.at[:, :, here], log_out.at[:, :, here], store_sem),
            ]

        def before(h, heads_of, here):
            return None

        def after(h, at, count, here, top, mixed, total, past):
            mix_ref[h, at : at + count, here, :] = (mixed / total).reshape(count, BLOCK, WIDTH)
            log_ref[h, at : at + count, here, :] = (top + jnp.log2(total)).reshape(count, BLOCK, WIDTH)

        def one_block(block, carry):
            here = chip * blocks + block
            low = jnp.maximum(document_start(doc_blocks, docs, here) - chip * blocks, 0)
            count = block - low + 1
            for width in range(3, blocks + 1, 3):
                @pl.when((count <= width) & (count > width - 3))
                def _():
                    start = block - width + 1
                    attend_block(width, heads, query_ref, pair_ref, block, pad + start * BLOCK, start, low, True,
                                 before, after)
            for copy in stores(block):
                copy.start()
            return carry

        lax.fori_loop(0, blocks, one_block, 0)

        def finish(block, carry):
            for copy in stores(block):
                copy.wait()
            return carry

        lax.fori_loop(0, blocks, finish, 0)

    state = jax.ShapeDtypeStruct((heads, GROUP, 2 * tokens, WIDTH), jnp.float32)
    return pl.pallas_call(
        kernel,
        out_shape=(state, state),
        in_specs=[SCALAR, SCALAR] + [HBM] * 4,
        out_specs=(ANY, ANY),
        scratch_shapes=[
            pltpu.VMEM((2 * tokens, heads * GROUP * WIDTH), jnp.bfloat16),
            pltpu.VMEM((pad + 2 * tokens, 2 * heads * WIDTH), jnp.bfloat16),
            pltpu.VMEM(state.shape, jnp.float32),
            pltpu.VMEM(state.shape, jnp.float32),
            pltpu.SemaphoreType.DMA(()),
            pltpu.SemaphoreType.DMA(()),
        ],
        compiler_params=pltpu.CompilerParams(vmem_limit_bytes=20 << 20),
        cost_estimate=pl.CostEstimate(flops=heads * 3_000_000_000, transcendentals=0, bytes_accessed=8_000_000),
    )


def far_call(first, heads, tokens, docs, whole, carried):
    blocks = 2 * tokens // BLOCK
    slots = 3 if whole else 2
    states_in = 0 if whole else 2

    def kernel(place, doc_blocks, queries, partner_queries, *rest):
        state_in, rest = rest[:states_in], rest[states_in:]
        pieces, rest = rest[: 2 * slots], rest[2 * slots + carried :]
        out, out_partner, query_ref, pair_ref, done_ref, load_sem, store_sem, *rest = rest
        state_refs, state_sem = rest[:states_in], rest[-1]
        chip = place[0] // 2
        core = place[0] % 2
        columns = pl.ds(aligned((core * HALF + first) * GROUP * WIDTH), heads * GROUP * WIDTH)
        loads = query_loads(queries, partner_queries, query_ref, place, first, heads, tokens, load_sem)
        for n, piece in enumerate(pieces):
            row = aligned((2 * (n // 2) + (core if n % 2 == 0 else 1 - core)) * tokens)
            loads.append(pltpu.make_async_copy(piece, pair_ref.at[pl.ds(row, tokens)], load_sem))

        def states(block):
            here = pl.ds(aligned(block * BLOCK), BLOCK)
            return [
                pltpu.make_async_copy(source.at[:, :, here], target.at[:, :, here], state_sem.at[block])
                for source, target in zip(state_in, state_refs)
            ]

        def store(block):
            here = pl.ds(aligned(block * BLOCK), BLOCK)
            own = block // (blocks // 2) == core
            to = pl.ds(aligned(block % (blocks // 2) * BLOCK), BLOCK)
            mine = pltpu.make_async_copy(done_ref.at[here], out.at[to, columns], store_sem)
            other = pltpu.make_async_copy(done_ref.at[here], out_partner.at[to], store_sem)
            return own, mine, other

        for copy in loads:
            copy.start()
        for block in range(blocks):
            for copy in states(block):
                copy.start()
        for copy in loads:
            copy.wait()

        def before(h, heads_of, here):
            rows = (heads_of.stop - heads_of.start) * BLOCK
            return None if whole else [ref[h, heads_of, here, :].reshape(rows, WIDTH) for ref in state_refs]

        def after(h, at, count, here, top, mixed, total, past):
            if not whole:
                factor = jnp.exp2(past[1] - top)
                mixed, total = past[0] * factor + mixed, total + factor
            done = (mixed / total).astype(jnp.bfloat16)
            for a in range(count):
                done_ref[here, pl.ds((h * GROUP + at + a) * WIDTH, WIDTH)] = done[a * BLOCK : (a + 1) * BLOCK]

        def one_block(block, carry):
            for copy in states(block):
                copy.wait()
            low = document_start(doc_blocks, docs, chip * blocks + block) - (chip - 2) * blocks
            end = 2 * blocks + block + 1 if whole else 2 * blocks
            count = end - low
            least = 0
            for width in range(2, LONGEST + 1, 2):
                @pl.when((count <= width) & (count > least))
                def _():
                    start = end - width
                    attend_block(width, heads, query_ref, pair_ref, block, start * BLOCK, start, low, whole,
                                 before, after)
                least = width

            if not whole:
                @pl.when(count <= 0)
                def _():
                    here = pl.ds(aligned(block * BLOCK), BLOCK)
                    for h in range(heads):
                        for a in range(GROUP):
                            done_ref[here, pl.ds((h * GROUP + a) * WIDTH, WIDTH)] = (
                                state_refs[0][h, a, here, :].astype(jnp.bfloat16))

            own, mine, other = store(block)

            @pl.when(own)
            def _():
                mine.start()

            @pl.when(jnp.logical_not(own))
            def _():
                other.start()

            return carry

        lax.fori_loop(0, blocks, one_block, 0)

        def finish(block, carry):
            own, mine, other = store(block)

            @pl.when(own)
            def _():
                mine.wait()

            @pl.when(jnp.logical_not(own))
            def _():
                other.wait()

            return carry

        lax.fori_loop(0, blocks, finish, 0)

    state = (heads, GROUP, 2 * tokens, WIDTH)
    return pl.pallas_call(
        kernel,
        out_shape=(
            jax.ShapeDtypeStruct((tokens, KEY_HEADS * GROUP * WIDTH), jnp.bfloat16),
            jax.ShapeDtypeStruct((tokens, heads * GROUP * WIDTH), jnp.bfloat16),
        ),
        in_specs=[SCALAR, SCALAR, HBM, HBM] + [ANY] * (states_in + 2 * slots + carried),
        out_specs=(ANY, ANY),
        scratch_shapes=[
            pltpu.VMEM((2 * tokens, heads * GROUP * WIDTH), jnp.bfloat16),
            pltpu.VMEM((2 * slots * tokens, 2 * heads * WIDTH), jnp.bfloat16),
            pltpu.VMEM((2 * tokens, heads * GROUP * WIDTH), jnp.bfloat16),
            pltpu.SemaphoreType.DMA(()),
            pltpu.SemaphoreType.DMA(()),
        ] + [pltpu.VMEM(state, jnp.float32)] * states_in + [pltpu.SemaphoreType.DMA((blocks,))],
        input_output_aliases={4 + states_in + 2 * slots: 0} if carried else {},
        compiler_params=pltpu.CompilerParams(vmem_limit_bytes=28 << 20),
        cost_estimate=pl.CostEstimate(flops=heads * 4_000_000_000, transcendentals=0, bytes_accessed=8_000_000),
    )


def last_call(tokens, heads):
    width = heads * GROUP * WIDTH

    def kernel(place, out_in, *rest):
        *returned, out, sem = rest
        copies = []
        for part, source in enumerate(returned):
            other = aligned(((1 - place[0] % 2) * HALF + part * heads) * GROUP * WIDTH)
            copies.append(pltpu.make_async_copy(source, out.at[:, pl.ds(other, width)], sem.at[part]))
            copies[part].start()
        for copy in copies:
            copy.wait()

    return pl.pallas_call(
        kernel,
        out_shape=jax.ShapeDtypeStruct((tokens, KEY_HEADS * GROUP * WIDTH), jnp.bfloat16),
        in_specs=[SCALAR, ANY] + [pl.BlockSpec(memory_space=pltpu.VMEM)] * (HALF // heads),
        out_specs=ANY,
        scratch_shapes=[pltpu.SemaphoreType.DMA((HALF // heads,))],
        input_output_aliases={1: 0},
        compiler_params=pltpu.CompilerParams(vmem_limit_bytes=8 << 20),
    )


def on_device(queries, keys, values, doc_blocks):
    tokens = queries.shape[0]
    docs = doc_blocks.shape[0]
    place = lax.axis_index("ctx").astype(jnp.int32)
    odd = (place // 2) % 2 == 1
    place = place.reshape(1)
    swap = lambda x: permuted(x, lambda i: i ^ 1)
    hop = lambda x: permuted(x, lambda i: i + 4)
    across = lambda x: permuted(x, lambda i: i ^ 2)

    other, own, other_late, own_late = pack_call(tokens, 2)(place, keys, values)
    received = swap(other)
    received_late = swap(other_late)
    partner_queries = swap(queries)
    near = [own, received, own_late, received_late]
    common = (place, doc_blocks, queries, partner_queries)
    relay = lambda n: across(jnp.where(odd, far[n], near[n]))
    far = [hop(x) for x in near[:2]]
    before = [relay(0)]
    late = near[2]
    far.append(hop(late))
    before.append(relay(1))
    last, far[1] = lax.optimization_barrier((near[3], far[1]))
    final, before[0] = lax.optimization_barrier((near[3], before[0]))
    before[0], far[2] = lax.optimization_barrier((before[0], far[2]))
    before.append(relay(2))
    far.append(hop(last))
    before.append(permuted(final, lambda i: i + 2))
    before[1], far[2] = lax.optimization_barrier((before[1], far[2]))
    out, partner = far_call(0, 2, tokens, docs, True, False)(*common, *far[:2], *before[:2], *near[:2])
    out, partner_late = far_call(2, 2, tokens, docs, True, True)(*common, *far[2:], *before[2:], *near[2:], out)
    return last_call(tokens, 2)(place, out, swap(partner), swap(partner_late))


def solution(mesh):
    placed = (
        P(("groups", "ctx"), None),
        P(("groups", "ctx"), None),
        P(("groups", "ctx"), None),
        P("groups"),
    )
    return jax.shard_map(
        on_device, mesh=mesh, in_specs=placed, out_specs=P(("groups", "ctx"), None), check_vma=False
    )
```
